32 devices in a mesh: scan: 8 (over z, x), depth: 4 (over y, core).
Axes of the slice: x: 2, y: 2, z: 4, core: 2. Of those that a mesh axis runs over, the one named last changes fastest.
Arguments:
- object_slices: float32 [4, 2, 512, 2048], P('depth', None, 'scan'), may hold values from -1 to 1, as said below
- probe_wave: float32 [2, 128, 128], replicated, may hold values from -4 to 4
- offsets: int32 [128, 2], P('scan'), may hold values from 0 to 1920, as said below
- intensity: float32 [128, 128, 128], P('scan'), may hold values from 0 to 1
Outputs:
- gradient: float32 [4, 2, 512, 2048], P('depth', None, 'scan')
The draws below stay inside these ranges and needn't reach their ends.
Inputs may be any that keep to these rules, and one draw needn't show every extreme that they name: `offsets`: position k has its row offset between max(0, (k // 16) * 64 - 64) and min(384, (k // 16) * 64 + 2 * 64 - 128), both ends reached on every scan device, and its column offset between 0 and 1920, both reached on every scan device. `object_slices`: each entry has magnitude at most 1.
All inputs are finite; a program needn't handle non-finite values.
Results may differ from the reference program's by a relative error of at most 0.007.
Values may be sent and summed in bfloat16 or wider, within the bound.
A program may use at most 64 MiB of HBM per device.

```python
import math
import jax
import jax.numpy as jnp
from jax import lax

WAVE = 128
STRIP = 64
NX = 2048
POS_DEV = 16
SLICES = 4
NY = 512
POS = 128


def draw_object_slices(key, part):
    amplitude_key, phase_key = jax.random.split(jax.random.fold_in(key, 11))
    amplitude = jax.random.uniform(amplitude_key, (SLICES, NY, NX), jnp.float32, 0.93, 1.0)
    phase_values = jax.random.uniform(phase_key, (SLICES, NY, NX), jnp.float32, -math.pi, math.pi)
    return jnp.stack([amplitude * jnp.cos(phase_values), amplitude * jnp.sin(phase_values)], axis=1)


def draw_offsets(key, part):
    row_key, col_key = jax.random.split(jax.random.fold_in(key, 23))
    position_index = jnp.arange(POS, dtype=jnp.int32)
    owner_index = position_index // POS_DEV
    row_low = jnp.maximum(0, owner_index * STRIP - STRIP)
    row_high = jnp.minimum(NY - WAVE, owner_index * STRIP + 2 * STRIP - WAVE)
    row_starts = row_low + jax.random.randint(row_key, (POS,), 0, row_high - row_low + 1)
    rank_in_device = position_index % POS_DEV
    row_starts = jnp.where(rank_in_device == 0, row_high, jnp.where(rank_in_device == 1, row_low, row_starts))
    col_starts = jax.random.randint(col_key, (POS,), 0, NX - WAVE + 1)
    col_starts = jnp.where(rank_in_device == 0, NX - WAVE, jnp.where(rank_in_device == 1, 0, col_starts))
    return jnp.stack([row_starts, col_starts], axis=1).astype(jnp.int32)


def steps_of(rng, dims, pieces, low, largest):
    loudness = 1.0
    for axis_at, blocks in pieces:
        heights = jax.random.uniform(jax.random.fold_in(jax.random.fold_in(rng, 6), axis_at), (blocks,), jnp.float32, low / len(pieces), largest / len(pieces))
        loudness = loudness * jnp.repeat(jnp.exp(heights), dims[axis_at] // blocks).reshape((-1,) + (1,) * (len(dims) - 1 - axis_at))
    return loudness


def gaussian(stream_key, dims, deviation, limit, held_as=jnp.bfloat16):
    entries = deviation * jax.random.normal(stream_key, dims, jnp.float32)
    return jnp.clip(entries, min=-limit, max=limit).astype(held_as)


def setup_inputs(seed: int = 0) -> dict:
    key_list = jax.random.split(jax.random.key(seed), 5)
    return {
        "object_slices": draw_object_slices(jax.random.fold_in(key_list[4], 71), 0),
        "probe_wave": gaussian(key_list[1], (2, WAVE, WAVE), 0.7, 4.0, jnp.float32),
        "offsets": draw_offsets(jax.random.fold_in(key_list[4], 71), 0),
        "intensity": jnp.clip(1.0 * jax.random.uniform(key_list[3], (POS, WAVE, WAVE), jnp.float32) ** steps_of(key_list[3], (POS, WAVE, WAVE), ((0, 8),), -0.2, 0.2), 0.0, 1.0),
    }


FRESNEL = 0.0024
HIGHEST = lax.Precision.HIGHEST

def transform_tables(extent):
    position_index = jnp.arange(extent, dtype=jnp.int32)
    product = position_index[:, None] * position_index[None, :] % extent
    phases = -2.0 * math.pi / extent * product.astype(jnp.float32)
    scaling = 1.0 / math.sqrt(extent)
    return (jnp.cos(phases) * scaling, jnp.sin(phases) * scaling)

def kernel_table(extent):
    position_index = jnp.arange(extent, dtype=jnp.int32)
    signed = jnp.where(position_index < extent // 2, position_index, position_index - extent).astype(jnp.float32)
    square = signed * signed
    phases = -math.pi * FRESNEL * (square[:, None] + square[None, :])
    return jnp.stack([jnp.cos(phases), jnp.sin(phases)], axis=0)[None]

def left_product(matrix, field_in):
    real_part, imag_part = (field_in[:, 0], field_in[:, 1])
    out_real = jnp.einsum('jk,bkl->bjl', matrix[0], real_part, precision=HIGHEST) - jnp.einsum('jk,bkl->bjl', matrix[1], imag_part, precision=HIGHEST)
    out_imag = jnp.einsum('jk,bkl->bjl', matrix[0], imag_part, precision=HIGHEST) + jnp.einsum('jk,bkl->bjl', matrix[1], real_part, precision=HIGHEST)
    return jnp.stack([out_real, out_imag], axis=1)

def right_product(field_in, matrix):
    real_part, imag_part = (field_in[:, 0], field_in[:, 1])
    out_real = jnp.einsum('bjk,kl->bjl', real_part, matrix[0], precision=HIGHEST) - jnp.einsum('bjk,kl->bjl', imag_part, matrix[1], precision=HIGHEST)
    out_imag = jnp.einsum('bjk,kl->bjl', imag_part, matrix[0], precision=HIGHEST) + jnp.einsum('bjk,kl->bjl', real_part, matrix[1], precision=HIGHEST)
    return jnp.stack([out_real, out_imag], axis=1)

def spectrum(field_in, matrix):
    return right_product(left_product(matrix, field_in), matrix)

def complex_times(first, second):
    out_real = first[:, 0] * second[:, 0] - first[:, 1] * second[:, 1]
    out_imag = first[:, 0] * second[:, 1] + first[:, 1] * second[:, 0]
    return jnp.stack([out_real, out_imag], axis=1)

def conjugate(field_in):
    return jnp.stack([field_in[:, 0], -field_in[:, 1]], axis=1)

def propagate(field_in, forward, backward, kernel):
    return spectrum(complex_times(spectrum(field_in, forward), kernel), backward)

def retreat(field_in, forward, backward, kernel):
    return spectrum(complex_times(spectrum(field_in, backward), conjugate(kernel)), forward)

def reference(object_slices, probe_wave, offsets, intensity):
    extent = probe_wave.shape[-1]
    forward = transform_tables(extent)
    backward = (forward[0], -forward[1])
    kernel = kernel_table(extent)
    positions = offsets.shape[0]
    window_span = jnp.arange(extent, dtype=jnp.int32)
    row_index = offsets[:, 0][:, None, None] + window_span[None, :, None]
    col_index = offsets[:, 1][:, None, None] + window_span[None, None, :]

    def cut_patches(layer_in):
        return jnp.moveaxis(layer_in[:, row_index, col_index], 0, 1)
    wave_in = jnp.broadcast_to(probe_wave, (positions,) + probe_wave.shape).astype(jnp.float32)
    entered = []
    excited = wave_in
    for slice_index in range(SLICES):
        entered.append(wave_in)
        excited = complex_times(cut_patches(object_slices[slice_index]), wave_in)
        if slice_index < SLICES - 1:
            propagated = propagate(excited, forward, backward, kernel).astype(jnp.bfloat16)
            wave_in = lax.optimization_barrier(propagated).astype(jnp.float32)
    far_field = spectrum(excited, forward)
    misfit = far_field[:, 0] * far_field[:, 0] + far_field[:, 1] * far_field[:, 1] - intensity
    adjoint = spectrum(far_field * misfit[:, None], backward)
    gradients = [None] * SLICES
    for slice_index in range(SLICES - 1, -1, -1):
        contribution = complex_times(conjugate(entered[slice_index]), adjoint)
        empty = jnp.zeros(object_slices.shape[1:], jnp.float32)
        gradients[slice_index] = empty.at[:, row_index, col_index].add(jnp.moveaxis(contribution, 1, 0))
        if slice_index > 0:
            masked = complex_times(conjugate(cut_patches(object_slices[slice_index])), adjoint)
            propagated = retreat(masked, forward, backward, kernel).astype(jnp.bfloat16)
            adjoint = lax.optimization_barrier(propagated).astype(jnp.float32)
    return jnp.stack(gradients, axis=0)
```

```python
import functools
import math

import jax
import jax.numpy as jnp
import numpy as np
from jax import lax
from jax.experimental import pallas as pl
from jax.experimental.pallas import tpu as pltpu
from jax.sharding import PartitionSpec as P

FRESNEL = 0.0024
MESH = pl.DeviceIdType.MESH
HOP, HOP_CONJ, FOURIER, FOURIER_CONJ = range(4)
CONJUGATE_OF = {HOP: HOP_CONJ, HOP_CONJ: HOP, FOURIER: FOURIER_CONJ, FOURIER_CONJ: FOURIER}


def block_tables(extent):
    index = np.arange(extent)
    fourier = np.exp(-2j * math.pi / extent * (index[:, None] * index[None, :] % extent))
    fourier = fourier / math.sqrt(extent)
    signed = np.where(index < extent // 2, index, index - extent).astype(np.float64)
    phase = np.exp(-1j * math.pi * FRESNEL * signed * signed)
    hop = (fourier.conj() * phase[None, :]) @ fourier
    tables = []
    for matrix in (hop, hop.conj(), fourier, fourier.conj()):
        real, imag = (matrix.real, matrix.imag)
        block = np.block([[real, imag], [-imag, real]]).astype(np.float32)
        high = block.astype(jnp.bfloat16)
        tables.append(np.stack([high, (block - high.astype(np.float32)).astype(jnp.bfloat16)]))
    return np.stack(tables)


def times(first, second):
    return (
        first[0] * second[0] - first[1] * second[1],
        first[0] * second[1] + first[1] * second[0],
    )


def conj_times(first, second):
    return (
        first[0] * second[0] + first[1] * second[1],
        first[0] * second[1] - first[1] * second[0],
    )


def split(value):
    high = value.astype(jnp.bfloat16)
    return high, (value - high.astype(jnp.float32)).astype(jnp.bfloat16)


def dot(first, second):
    return jnp.dot(first, second, preferred_element_type=jnp.float32)


def right_product(fields, high, low):
    extent = fields[0][0].shape[1]
    rows = [jnp.concatenate(field, axis=1) for field in fields]
    value_high, value_low = split(jnp.concatenate(rows, axis=0))
    out = dot(value_high, high) + dot(value_low, high) + dot(value_high, low)
    picks = [slice(i * extent, (i + 1) * extent) for i in range(len(fields))]
    return [(out[pick, :extent], out[pick, extent:]) for pick in picks]


def left_product(fields, high, low):
    extent = fields[0][0].shape[0]
    columns = [jnp.concatenate(field, axis=0) for field in fields]
    value_high, value_low = split(jnp.concatenate(columns, axis=1))
    if len(fields) == 1:
        both = dot(high, jnp.concatenate([value_high, value_low], axis=1))
        out = both[:, :extent] + both[:, extent:] + dot(low, value_high)
    else:
        out = dot(high, value_high) + dot(high, value_low) + dot(low, value_high)
    picks = [slice(i * extent, (i + 1) * extent) for i in range(len(fields))]
    return [(out[:extent, pick], out[extent:, pick]) for pick in picks]


def transform(fields, tables_ref, kind):
    other = CONJUGATE_OF[kind]
    fields = right_product(fields, tables_ref[kind, 0], tables_ref[kind, 1])
    return left_product(fields, tables_ref[other, 0], tables_ref[other, 1])


def column_blocks(column, extent, columns):
    block = column // extent
    following = jnp.minimum(block + 1, columns // extent - 1)
    first = pl.multiple_of(block * extent, extent)
    return first, pl.multiple_of(following * extent, extent), column - block * extent


def kept_rows(shape, row, above):
    inside = lax.broadcasted_iota(jnp.int32, shape, 0) >= row
    return inside.astype(jnp.int32) == above


def exchange_kernel(
    sections,
    peers,
    batch,
    offsets_ref,
    layer_hbm,
    probe_hbm,
    intensity_hbm,
    tables_hbm,
    own_terms,
    near_terms,
    far_terms,
    near_places,
    far_places,
    layer,
    probe,
    intensity,
    tables,
    own_out,
    own_in,
    relay_out,
    relay_in,
    joined,
    rim_in,
    own_back,
    rim_back,
    waves,
    adjoint,
    layer_sems,
    load_sems,
    place_send,
    place_recv,
    own_send,
    own_recv,
    relay_send,
    relay_recv,
    rim_send,
    rim_recv,
    own_back_send,
    own_back_recv,
    rim_back_send,
    rim_back_recv,
    onward_send,
    onward_recv,
):
    section = lax.axis_index("depth")
    scan = lax.axis_index("scan")
    even = jnp.where(lax.rem(scan, 2) == 0, 1, 0)
    odd = 1 - even
    partner = scan + even - odd
    far = scan - even + odd
    outward = scan - 2 * even + 2 * odd
    inward = scan + 2 * even - 2 * odd
    has_outward = (outward >= 0) & (outward < peers)
    has_inward = (inward >= 0) & (inward < peers)
    blocks, _, strip, extent = layer.shape
    owned = intensity.shape[0]
    groups = owned // batch

    loads = [
        pltpu.make_async_copy(source, target, load_sems.at[i])
        for i, (source, target) in enumerate(
            (
                (probe_hbm, probe),
                (intensity_hbm.at[pl.ds(section * owned, owned)], intensity),
                (tables_hbm, tables),
            )
        )
    ]

    def layer_load(block):
        columns = pl.ds(pl.multiple_of(block * extent, extent), extent)
        return pltpu.make_async_copy(
            layer_hbm.at[:, :, columns], layer.at[block], layer_sems.at[block]
        )

    def start_layer(block, carry):
        layer_load(block).start()
        return carry

    lax.fori_loop(0, blocks, start_layer, 0)
    for load in loads:
        load.start()

    barrier = pltpu.get_barrier_semaphore()

    def greet(**device):
        pl.semaphore_signal(barrier, inc=1, device_id=device, device_id_type=MESH)

    def greet_section(step, carry):
        other = lax.rem(section + step, sections)
        greet(scan=partner, depth=other)

        @pl.when(step > 0)
        def _():
            greet(depth=other)

        return carry

    lax.fori_loop(0, sections, greet_section, 0)

    @pl.when(has_outward)
    def _():
        greet(scan=outward)
        greet(scan=far)

    @pl.when(jnp.logical_not(has_outward))
    def _():
        far_terms[...] = jnp.zeros_like(far_terms)

    @pl.when(has_inward)
    def _():
        greet(scan=inward)

    @pl.when(jnp.logical_not(has_inward))
    def _():
        relay_in[...] = jnp.zeros_like(relay_in)

    greeted = 2 * sections - 1 + jnp.where(has_outward, 2, 0) + jnp.where(has_inward, 1, 0)
    pl.semaphore_wait(barrier, greeted)

    def remote(source, target, send, recv, device):
        return pltpu.make_async_remote_copy(
            src_ref=source,
            dst_ref=target,
            send_sem=send,
            recv_sem=recv,
            device_id=device,
            device_id_type=MESH,
        )

    near_place_copy = remote(
        offsets_ref, near_places, place_send.at[0], place_recv.at[0], {"scan": partner}
    )
    far_place_copy = remote(
        offsets_ref, far_places, place_send.at[1], place_recv.at[1], {"scan": far}
    )
    near_place_copy.start()

    @pl.when(has_outward)
    def _():
        far_place_copy.start()

    @pl.when(jnp.logical_not(has_outward))
    def _():
        def clear(index, carry):
            far_places[0, index] = 0
            far_places[1, index] = 0
            return carry

        lax.fori_loop(0, far_places.shape[1], clear, 0)

    def of_owner(owner, group):
        return pl.ds(owner * owned + group * batch, batch)

    def of_group(group):
        return pl.ds(group * batch, batch)

    def own_copy(owner, sender, group):
        return remote(
            own_out.at[of_owner(owner, group)],
            own_in.at[sender, of_group(group)],
            own_send.at[owner, group],
            own_recv.at[sender, group],
            {"depth": owner},
        )

    def relay_copy(owner, group):
        place = of_owner(owner, group)
        return remote(
            relay_out.at[place],
            relay_in.at[place],
            relay_send.at[owner, group],
            relay_recv.at[owner, group],
            {"scan": outward},
        )

    def rim_copy(owner, sender, group):
        return remote(
            joined.at[of_owner(owner, group)],
            rim_in.at[sender, of_group(group)],
            rim_send.at[owner, group],
            rim_recv.at[sender, group],
            {"scan": partner, "depth": owner},
        )

    def own_back_copy(target, sender, group):
        return remote(
            own_back.at[target, of_group(group)],
            own_terms.at[of_owner(sender, group)],
            own_back_send.at[target, group],
            own_back_recv.at[sender, group],
            {"depth": target},
        )

    def rim_back_copy(target, sender, group):
        return remote(
            rim_back.at[target, of_group(group)],
            near_terms.at[of_owner(sender, group)],
            rim_back_send.at[target, group],
            rim_back_recv.at[sender, group],
            {"scan": partner, "depth": target},
        )

    def onward_copy(owner, group):
        place = of_owner(owner, group)
        return remote(
            near_terms.at[place],
            far_terms.at[place],
            onward_send.at[owner, group],
            onward_recv.at[owner, group],
            {"scan": inward},
        )

    lanes = lax.broadcasted_iota(jnp.int32, (strip, extent), 1)

    def cut(column, part):
        first = column // extent
        second = jnp.minimum(first + 1, blocks - 1)
        return jnp.where(lanes >= lax.rem(column, extent), layer[first, part], layer[second, part])

    def each_message(body):
        def step(index, carry):
            body(lax.rem(section + 1 + index % sections, sections), index // sections)
            return carry

        lax.fori_loop(0, sections * groups, step, 0)

    def wait_layer(block, carry):
        layer_load(block).wait()
        return carry

    lax.fori_loop(0, blocks, wait_layer, 0)

    def send_own(owner, group):
        for item in range(batch):
            index = owner * owned + group * batch + item
            for part in range(2):
                half = cut(offsets_ref[1, index], part).astype(jnp.bfloat16)
                own_out[index, part] = half

        @pl.when(owner != section)
        def _():
            own_copy(owner, section, group).start()

        @pl.when(owner == section)
        def _():
            own_in[section, of_group(group)] = own_out[of_owner(section, group)]

    each_message(send_own)

    @pl.when(has_outward)
    def _():
        far_place_copy.wait()

        def send_relay(owner, group):
            for item in range(batch):
                index = owner * owned + group * batch + item
                row = far_places[0, index] - (far - 1) * strip
                keep = kept_rows((strip, extent), row, odd)
                for part in range(2):
                    half = jnp.where(keep, cut(far_places[1, index], part), 0.0)
                    relay_out[index, part] = half.astype(jnp.bfloat16)
            relay_copy(owner, group).start()

        each_message(send_relay)

    near_place_copy.wait()

    def send_rim(owner, group):
        @pl.when(has_inward)
        def _():
            relay_copy(owner, group).wait_recv()

        for item in range(batch):
            index = owner * owned + group * batch + item
            row = near_places[0, index] - (partner - 1) * strip
            keep = kept_rows((strip, extent), row, even)
            for part in range(2):
                passed = relay_in[index, part].astype(jnp.float32)
                half = jnp.where(keep, cut(near_places[1, index], part), passed)
                joined[index, part] = half.astype(jnp.bfloat16)
        rim_copy(owner, section, group).start()

    each_message(send_rim)
    for load in loads:
        load.wait()

    def patch(slice_index, index):
        return tuple(
            jnp.concatenate(
                [own_in[slice_index, index, part], rim_in[slice_index, index, part]], axis=0
            ).astype(jnp.float32)
            for part in range(2)
        )

    def stored(ref, *place):
        return (ref[(*place, 0)], ref[(*place, 1)])

    items = range(batch)
    final = sections - 1

    def onward(owner, group):
        rim_back_copy(section, owner, group).wait_recv()

        @pl.when(has_inward)
        def _():
            onward_copy(owner, group).start()

    def entering(group):
        for item in items:
            index = section * owned + group * batch + item
            down = offsets_ref[0, index] - (scan - 1) * strip + strip
            right = lax.rem(offsets_ref[1, index], extent)
            for part in range(2):
                rolled = pltpu.roll(probe[part], lax.rem(down, extent), 0)
                waves[0, item, part] = pltpu.roll(rolled, right, 1)

    def excite(slice_index, group):
        @pl.when(slice_index != section)
        def _():
            own_copy(section, slice_index, group).wait_recv()

        rim_copy(section, slice_index, group).wait_recv()
        return [
            times(patch(slice_index, group * batch + item), stored(waves, slice_index, item))
            for item in items
        ]

    def run_group(group, carry):
        entering(group)

        def forward(slice_index, inner):
            result = transform(excite(slice_index, group), tables, HOP)
            for item in items:
                for part in range(2):
                    waves[slice_index + 1, item, part] = result[item][part]
            return inner

        lax.fori_loop(0, final, forward, 0)
        fields = transform(excite(final, group), tables, FOURIER)
        driven = []
        for item in items:
            real, imag = fields[item]
            misfit = real * real + imag * imag - intensity[group * batch + item]
            driven.append((misfit * real, misfit * imag))
        fields = transform(driven, tables, FOURIER_CONJ)
        for item in items:
            for part in range(2):
                adjoint[item, part] = fields[item][part]

        def give(slice_index):
            for item in items:
                index = group * batch + item
                term = conj_times(stored(waves, slice_index, item), stored(adjoint, item))
                for part in range(2):
                    value = term[part].astype(jnp.bfloat16)
                    own_back[slice_index, index, part] = value[:strip]
                    rim_back[slice_index, index, part] = value[strip:]
            rim_back_copy(slice_index, section, group).start()

            @pl.when(slice_index != section)
            def _():
                own_back_copy(slice_index, section, group).start()

            @pl.when(slice_index == section)
            def _():
                own_terms[of_owner(section, group)] = own_back[section, of_group(group)]

        def backward(step, inner):
            slice_index = final - step
            give(slice_index)
            masked = [
                conj_times(patch(slice_index, group * batch + item), stored(adjoint, item))
                for item in items
            ]
            result = transform(masked, tables, HOP_CONJ)
            for item in items:
                for part in range(2):
                    adjoint[item, part] = result[item][part]

            @pl.when(group > 0)
            def _():
                onward(step, group - 1)

            return inner

        lax.fori_loop(0, final, backward, 0)
        give(0)

        @pl.when(group > 0)
        def _():
            onward(final, group - 1)

        return carry

    lax.fori_loop(0, groups, run_group, 0)

    def onward_last(owner, carry):
        onward(owner, groups - 1)
        return carry

    lax.fori_loop(0, sections, onward_last, 0)

    def drain(owner, group):
        rim_copy(owner, section, group).wait_send()
        rim_back_copy(owner, section, group).wait_send()

        @pl.when(owner != section)
        def _():
            own_copy(owner, section, group).wait_send()
            own_back_copy(owner, section, group).wait_send()
            own_back_copy(section, owner, group).wait_recv()

        @pl.when(has_outward)
        def _():
            relay_copy(owner, group).wait_send()
            onward_copy(owner, group).wait_recv()

        @pl.when(has_inward)
        def _():
            onward_copy(owner, group).wait_send()

    each_message(drain)


def exchange(sections, peers, offsets, layer, probe, intensity):
    positions, extent = (intensity.shape[0], intensity.shape[-1])
    strip, columns = layer.shape[1:]
    blocks = columns // extent
    owned = positions // sections
    batch = 2 if owned % 2 == 0 else 1
    hbm = pl.BlockSpec(memory_space=pltpu.HBM)
    vmem = pl.BlockSpec(memory_space=pltpu.VMEM)
    smem = pl.BlockSpec(memory_space=pltpu.SMEM)
    tables = jnp.asarray(block_tables(extent))
    halves = (positions, 2, strip, extent)
    split_halves = (sections, owned, 2, strip, extent)
    flat, nested = (pltpu.VMEM(halves, jnp.bfloat16), pltpu.VMEM(split_halves, jnp.bfloat16))
    semaphores = pltpu.SemaphoreType.DMA((sections, owned // batch))
    return pl.pallas_call(
        functools.partial(exchange_kernel, sections, peers, batch),
        out_shape=[jax.ShapeDtypeStruct(halves, jnp.bfloat16)] * 3
        + [jax.ShapeDtypeStruct((2, positions), jnp.int32)] * 2,
        in_specs=[smem] + [hbm] * 4,
        out_specs=[vmem] * 3 + [smem] * 2,
        scratch_shapes=[
            pltpu.VMEM((blocks, 2, strip, extent), jnp.float32),
            pltpu.VMEM(probe.shape, jnp.float32),
            pltpu.VMEM((owned, extent, extent), jnp.float32),
            pltpu.VMEM(tables.shape, jnp.bfloat16),
            flat,
            nested,
            flat,
            flat,
            flat,
            nested,
            nested,
            nested,
            pltpu.VMEM((sections, batch, 2, extent, extent), jnp.float32),
            pltpu.VMEM((batch, 2, extent, extent), jnp.float32),
            pltpu.SemaphoreType.DMA((blocks,)),
            pltpu.SemaphoreType.DMA((3,)),
            pltpu.SemaphoreType.DMA((2,)),
            pltpu.SemaphoreType.DMA((2,)),
        ]
        + [semaphores] * 12,
        compiler_params=pltpu.CompilerParams(
            collective_id=0, has_side_effects=True, vmem_limit_bytes=56 * 1024 * 1024
        ),
        name="exchange",
    )(offsets, layer, probe, intensity, tables)


def scatter_kernel(
    scan_ref, offsets_ref, near_places, far_places, own_ref, near_ref, far_ref, out_ref
):
    scan = scan_ref[0]
    positions = own_ref.shape[0]
    strip, extent = own_ref.shape[2:]
    columns = out_ref.shape[2]
    even = jnp.where(lax.rem(scan, 2) == 0, 1, 0)
    odd = 1 - even
    partner = scan + even - odd
    far = scan - even + odd
    out_ref[...] = jnp.zeros_like(out_ref)
    lanes = lax.broadcasted_iota(jnp.int32, (strip, extent), 1)

    def add(source, index, column, keep):
        first, second, shift = column_blocks(column, extent, columns)
        ahead = lanes >= shift
        for part in range(2):
            term = source[index, part].astype(jnp.float32)
            if keep is not None:
                term = jnp.where(keep, term, 0.0)
            for start, value in (
                (first, jnp.where(ahead, term, 0.0)),
                (second, jnp.where(ahead, 0.0, term)),
            ):
                place = (part, slice(None), pl.ds(start, extent))
                out_ref[place] = out_ref[place] + value

    def step(index, carry):
        add(own_ref, index, offsets_ref[1, index], None)
        near_row = near_places[0, index] - (partner - 1) * strip
        keep = kept_rows((strip, extent), near_row, even)
        add(near_ref, index, near_places[1, index], keep)
        far_row = far_places[0, index] - (far - 1) * strip
        keep = kept_rows((strip, extent), far_row, odd)
        add(far_ref, index, far_places[1, index], keep)
        return carry

    lax.fori_loop(0, positions, step, 0)


def scatter(offsets, near_places, far_places, terms, strip, columns):
    smem = pl.BlockSpec(memory_space=pltpu.SMEM)
    vmem = pl.BlockSpec(memory_space=pltpu.VMEM)
    scan = lax.axis_index("scan").astype(jnp.int32).reshape(1)
    return pl.pallas_call(
        scatter_kernel,
        out_shape=jax.ShapeDtypeStruct((2, strip, columns), jnp.float32),
        in_specs=[smem] * 4 + [vmem] * 3,
        out_specs=vmem,
        compiler_params=pltpu.CompilerParams(vmem_limit_bytes=12 * 1024 * 1024),
        name="scatter",
    )(scan, offsets, near_places, far_places, *terms)


def shards(peers, sections, object_slices, probe_wave, offsets, intensity):
    layer = object_slices[0]
    strip, columns = layer.shape[1:]
    places = offsets.T
    *terms, near_places, far_places = exchange(
        sections, peers, places, layer, probe_wave, intensity
    )
    return scatter(places, near_places, far_places, terms, strip, columns)[None]


def solution(mesh):
    in_specs = (P("depth", None, "scan", None), P(), P("scan", None), P("scan", None, None))
    out_specs = P("depth", None, "scan", None)
    body = functools.partial(shards, mesh.shape["scan"], mesh.shape["depth"])
    return jax.shard_map(body, mesh=mesh, in_specs=in_specs, out_specs=out_specs, check_vma=False)
```

```python
import functools
import math

import jax
import jax.numpy as jnp
import numpy as np
from jax import lax
from jax.experimental import pallas as pl
from jax.experimental.pallas import tpu as pltpu
from jax.sharding import PartitionSpec as P

FRESNEL = 0.0024
MESH = pl.DeviceIdType.MESH
HOP, HOP_CONJ, FOURIER, FOURIER_CONJ = range(4)
CONJUGATE_OF = {HOP: HOP_CONJ, HOP_CONJ: HOP, FOURIER: FOURIER_CONJ, FOURIER_CONJ: FOURIER}


def block_tables(extent):
    index = np.arange(extent)
    fourier = np.exp(-2j * math.pi / extent * (index[:, None] * index[None, :] % extent))
    fourier = fourier / math.sqrt(extent)
    signed = np.where(index < extent // 2, index, index - extent).astype(np.float64)
    phase = np.exp(-1j * math.pi * FRESNEL * signed * signed)
    hop = (fourier.conj() * phase[None, :]) @ fourier
    tables = []
    for matrix in (hop, hop.conj(), fourier, fourier.conj()):
        real, imag = (matrix.real, matrix.imag)
        block = np.block([[real, imag], [-imag, real]]).astype(np.float32)
        high = block.astype(jnp.bfloat16)
        tables.append(np.stack([high, (block - high.astype(np.float32)).astype(jnp.bfloat16)]))
    return np.stack(tables)


def times(first, second):
    return (
        first[0] * second[0] - first[1] * second[1],
        first[0] * second[1] + first[1] * second[0],
    )


def conj_times(first, second):
    return (
        first[0] * second[0] + first[1] * second[1],
        first[0] * second[1] - first[1] * second[0],
    )


def split(value):
    high = value.astype(jnp.bfloat16)
    return high, (value - high.astype(jnp.float32)).astype(jnp.bfloat16)


def dot(first, second):
    return jnp.dot(first, second, preferred_element_type=jnp.float32)


def right_product(fields, high, low):
    extent = fields[0][0].shape[1]
    rows = [jnp.concatenate(field, axis=1) for field in fields]
    value_high, value_low = split(jnp.concatenate(rows, axis=0))
    out = dot(value_high, high) + dot(value_low, high) + dot(value_high, low)
    picks = [slice(i * extent, (i + 1) * extent) for i in range(len(fields))]
    return [(out[pick, :extent], out[pick, extent:]) for pick in picks]


def left_product(fields, high, low):
    extent = fields[0][0].shape[0]
    columns = [jnp.concatenate(field, axis=0) for field in fields]
    value_high, value_low = split(jnp.concatenate(columns, axis=1))
    if len(fields) == 1:
        both = dot(high, jnp.concatenate([value_high, value_low], axis=1))
        out = both[:, :extent] + both[:, extent:] + dot(low, value_high)
    else:
        out = dot(high, value_high) + dot(high, value_low) + dot(low, value_high)
    picks = [slice(i * extent, (i + 1) * extent) for i in range(len(fields))]
    return [(out[:extent, pick], out[extent:, pick]) for pick in picks]


def transform(fields, tables_ref, kind):
    other = CONJUGATE_OF[kind]
    fields = right_product(fields, tables_ref[kind, 0], tables_ref[kind, 1])
    return left_product(fields, tables_ref[other, 0], tables_ref[other, 1])


def column_blocks(column, extent, columns):
    block = column // extent
    following = jnp.minimum(block + 1, columns // extent - 1)
    first = pl.multiple_of(block * extent, extent)
    return first, pl.multiple_of(following * extent, extent), column - block * extent


def kept_rows(shape, row, above):
    inside = lax.broadcasted_iota(jnp.int32, shape, 0) >= row
    return inside.astype(jnp.int32) == above


def exchange_kernel(
    sections,
    peers,
    batch,
    offsets_ref,
    layer_hbm,
    probe_hbm,
    intensity_hbm,
    tables_hbm,
    own_terms,
    near_terms,
    far_terms,
    near_places,
    far_places,
    layer,
    probe,
    intensity,
    intensity_out,
    intensity_in,
    tables,
    own_out,
    own_in,
    relay_out,
    relay_in,
    joined,
    rim_in,
    own_back,
    rim_back,
    waves,
    adjoint,
    layer_sems,
    load_sems,
    place_send,
    place_recv,
    intensity_send,
    intensity_recv,
    own_send,
    own_recv,
    relay_send,
    relay_recv,
    rim_send,
    rim_recv,
    own_back_send,
    own_back_recv,
    rim_back_send,
    rim_back_recv,
    onward_send,
    onward_recv,
):
    section = lax.axis_index("depth")
    scan = lax.axis_index("scan")
    even = jnp.where(lax.rem(scan, 2) == 0, 1, 0)
    odd = 1 - even
    partner = scan + even - odd
    far = scan - even + odd
    outward = scan - 2 * even + 2 * odd
    inward = scan + 2 * even - 2 * odd
    has_outward = (outward >= 0) & (outward < peers)
    has_inward = (inward >= 0) & (inward < peers)
    blocks, _, strip, extent = layer.shape
    owned = intensity.shape[0]
    groups = owned // batch

    loads = [
        pltpu.make_async_copy(source, target, load_sems.at[i])
        for i, (source, target) in enumerate(
            (
                (probe_hbm, probe),
                (intensity_hbm.at[pl.ds(section * owned, owned)], intensity),
                (tables_hbm, tables),
            )
        )
    ]

    def layer_load(block):
        columns = pl.ds(pl.multiple_of(block * extent, extent), extent)
        return pltpu.make_async_copy(
            layer_hbm.at[:, :, columns], layer.at[block], layer_sems.at[block]
        )

    def start_layer(block, carry):
        layer_load(block).start()
        return carry

    lax.fori_loop(0, blocks, start_layer, 0)
    for load in loads:
        load.start()

    barrier = pltpu.get_barrier_semaphore()

    def greet(**device):
        pl.semaphore_signal(barrier, inc=1, device_id=device, device_id_type=MESH)

    def greet_section(step, carry):
        other = lax.rem(section + step, sections)
        greet(scan=partner, depth=other)

        @pl.when(step > 0)
        def _():
            greet(depth=other)

        return carry

    lax.fori_loop(0, sections, greet_section, 0)

    @pl.when(has_outward)
    def _():
        greet(scan=outward)
        greet(scan=far)

    @pl.when(jnp.logical_not(has_outward))
    def _():
        far_terms[...] = jnp.zeros_like(far_terms)

    @pl.when(has_inward)
    def _():
        greet(scan=inward)

    @pl.when(jnp.logical_not(has_inward))
    def _():
        relay_in[...] = jnp.zeros_like(relay_in)

    greeted = 2 * sections - 1 + jnp.where(has_outward, 2, 0) + jnp.where(has_inward, 1, 0)
    pl.semaphore_wait(barrier, greeted)

    def remote(source, target, send, recv, device):
        return pltpu.make_async_remote_copy(
            src_ref=source,
            dst_ref=target,
            send_sem=send,
            recv_sem=recv,
            device_id=device,
            device_id_type=MESH,
        )

    near_place_copy = remote(
        offsets_ref, near_places, place_send.at[0], place_recv.at[0], {"scan": partner}
    )
    far_place_copy = remote(
        offsets_ref, far_places, place_send.at[1], place_recv.at[1], {"scan": far}
    )
    near_place_copy.start()

    @pl.when(has_outward)
    def _():
        far_place_copy.start()

    @pl.when(jnp.logical_not(has_outward))
    def _():
        def clear(index, carry):
            far_places[0, index] = 0
            far_places[1, index] = 0
            return carry

        lax.fori_loop(0, far_places.shape[1], clear, 0)

    def of_owner(owner, group):
        return pl.ds(owner * owned + group * batch, batch)

    def of_group(group):
        return pl.ds(group * batch, batch)

    def own_copy(owner, sender, group):
        return remote(
            own_out.at[of_owner(owner, group)],
            own_in.at[sender, of_group(group)],
            own_send.at[owner, group],
            own_recv.at[sender, group],
            {"scan": partner, "depth": owner},
        )

    def intensity_copy(group):
        return remote(
            intensity_out.at[of_group(group)],
            intensity_in.at[of_group(group)],
            intensity_send.at[group],
            intensity_recv.at[group],
            {"scan": partner},
        )

    def relay_copy(owner, group):
        place = of_owner(owner, group)
        return remote(
            relay_out.at[place],
            relay_in.at[place],
            relay_send.at[owner, group],
            relay_recv.at[owner, group],
            {"scan": outward},
        )

    def rim_copy(owner, sender, group):
        return remote(
            joined.at[of_owner(owner, group)],
            rim_in.at[sender, of_group(group)],
            rim_send.at[owner, group],
            rim_recv.at[sender, group],
            {"depth": owner},
        )

    def own_back_copy(target, sender, group):
        return remote(
            own_back.at[target, of_group(group)],
            own_terms.at[of_owner(sender, group)],
            own_back_send.at[target, group],
            own_back_recv.at[sender, group],
            {"scan": partner, "depth": target},
        )

    def rim_back_copy(target, sender, group):
        return remote(
            rim_back.at[target, of_group(group)],
            near_terms.at[of_owner(sender, group)],
            rim_back_send.at[target, group],
            rim_back_recv.at[sender, group],
            {"depth": target},
        )

    def onward_copy(owner, group):
        place = of_owner(owner, group)
        return remote(
            near_terms.at[place],
            far_terms.at[place],
            onward_send.at[owner, group],
            onward_recv.at[owner, group],
            {"scan": inward},
        )

    lanes = lax.broadcasted_iota(jnp.int32, (strip, extent), 1)

    def cut(column, part):
        first = column // extent
        second = jnp.minimum(first + 1, blocks - 1)
        return jnp.where(lanes >= lax.rem(column, extent), layer[first, part], layer[second, part])

    def each_message(body):
        def step(index, carry):
            body(lax.rem(section + 1 + index % sections, sections), index // sections)
            return carry

        lax.fori_loop(0, sections * groups, step, 0)

    loads[1].wait()

    def wait_layer(block, carry):
        layer_load(block).wait()
        return carry

    lax.fori_loop(0, blocks, wait_layer, 0)

    def send_own(owner, group):
        for item in range(batch):
            index = owner * owned + group * batch + item
            for part in range(2):
                half = cut(offsets_ref[1, index], part).astype(jnp.bfloat16)
                own_out[index, part] = half

        own_copy(owner, section, group).start()

        @pl.when(owner == section)
        def _():
            values = intensity[of_group(group)]
            intensity_out[of_group(group)] = values.astype(jnp.bfloat16)
            intensity_copy(group).start()

    each_message(send_own)

    @pl.when(has_outward)
    def _():
        far_place_copy.wait()

        def send_relay(owner, group):
            for item in range(batch):
                index = owner * owned + group * batch + item
                row = far_places[0, index] - (far - 1) * strip
                keep = kept_rows((strip, extent), row, odd)
                for part in range(2):
                    half = jnp.where(keep, cut(far_places[1, index], part), 0.0)
                    relay_out[index, part] = half.astype(jnp.bfloat16)
            relay_copy(owner, group).start()

        each_message(send_relay)

    near_place_copy.wait()

    def send_rim(owner, group):
        @pl.when(has_inward)
        def _():
            relay_copy(owner, group).wait_recv()

        for item in range(batch):
            index = owner * owned + group * batch + item
            row = near_places[0, index] - (partner - 1) * strip
            keep = kept_rows((strip, extent), row, even)
            for part in range(2):
                passed = relay_in[index, part].astype(jnp.float32)
                half = jnp.where(keep, cut(near_places[1, index], part), passed)
                joined[index, part] = half.astype(jnp.bfloat16)

        @pl.when(owner != section)
        def _():
            rim_copy(owner, section, group).start()

        @pl.when(owner == section)
        def _():
            rim_in[section, of_group(group)] = joined[of_owner(section, group)]

    each_message(send_rim)
    loads[0].wait()
    loads[2].wait()

    def patch(slice_index, index):
        return tuple(
            jnp.concatenate(
                [own_in[slice_index, index, part], rim_in[slice_index, index, part]], axis=0
            ).astype(jnp.float32)
            for part in range(2)
        )

    def stored(ref, *place):
        return (ref[(*place, 0)], ref[(*place, 1)])

    items = range(batch)
    final = sections - 1

    def onward(owner, group):
        @pl.when(owner != section)
        def _():
            rim_back_copy(section, owner, group).wait_recv()

        @pl.when(has_inward)
        def _():
            onward_copy(owner, group).start()

    def entering(group):
        for item in items:
            index = section * owned + group * batch + item
            down = near_places[0, index] - (partner - 2) * strip
            right = lax.rem(near_places[1, index], extent)
            for part in range(2):
                rolled = pltpu.roll(probe[part], lax.rem(down, extent), 0)
                waves[0, item, part] = pltpu.roll(rolled, right, 1)

    def excite(slice_index, group):
        own_copy(section, slice_index, group).wait_recv()

        @pl.when(slice_index != section)
        def _():
            rim_copy(section, slice_index, group).wait_recv()

        return [
            times(patch(slice_index, group * batch + item), stored(waves, slice_index, item))
            for item in items
        ]

    def run_group(group, carry):
        entering(group)

        def forward(slice_index, inner):
            result = transform(excite(slice_index, group), tables, HOP)
            for item in items:
                for part in range(2):
                    waves[slice_index + 1, item, part] = result[item][part]
            return inner

        lax.fori_loop(0, final, forward, 0)
        fields = transform(excite(final, group), tables, FOURIER)
        intensity_copy(group).wait_recv()
        driven = []
        for item in items:
            real, imag = fields[item]
            misfit = real * real + imag * imag - intensity_in[group * batch + item].astype(jnp.float32)
            driven.append((misfit * real, misfit * imag))
        fields = transform(driven, tables, FOURIER_CONJ)
        for item in items:
            for part in range(2):
                adjoint[item, part] = fields[item][part]

        def give(slice_index):
            for item in items:
                index = group * batch + item
                term = conj_times(stored(waves, slice_index, item), stored(adjoint, item))
                for part in range(2):
                    value = term[part].astype(jnp.bfloat16)
                    own_back[slice_index, index, part] = value[:strip]
                    rim_back[slice_index, index, part] = value[strip:]
            own_back_copy(slice_index, section, group).start()

            @pl.when(slice_index != section)
            def _():
                rim_back_copy(slice_index, section, group).start()

            @pl.when(slice_index == section)
            def _():
                near_terms[of_owner(section, group)] = rim_back[section, of_group(group)]

        def backward(step, inner):
            slice_index = final - step
            give(slice_index)
            masked = [
                conj_times(patch(slice_index, group * batch + item), stored(adjoint, item))
                for item in items
            ]
            result = transform(masked, tables, HOP_CONJ)
            for item in items:
                for part in range(2):
                    adjoint[item, part] = result[item][part]

            @pl.when(group > 0)
            def _():
                onward(step, group - 1)

            return inner

        lax.fori_loop(0, final, backward, 0)
        give(0)

        @pl.when(group > 0)
        def _():
            onward(final, group - 1)

        return carry

    lax.fori_loop(0, groups, run_group, 0)

    def onward_last(owner, carry):
        onward(owner, groups - 1)
        return carry

    lax.fori_loop(0, sections, onward_last, 0)

    def drain(owner, group):
        own_copy(owner, section, group).wait_send()
        own_back_copy(owner, section, group).wait_send()
        own_back_copy(section, owner, group).wait_recv()

        @pl.when(owner != section)
        def _():
            rim_copy(owner, section, group).wait_send()
            rim_back_copy(owner, section, group).wait_send()

        @pl.when(owner == section)
        def _():
            intensity_copy(group).wait_send()

        @pl.when(has_outward)
        def _():
            relay_copy(owner, group).wait_send()
            onward_copy(owner, group).wait_recv()

        @pl.when(has_inward)
        def _():
            onward_copy(owner, group).wait_send()

    each_message(drain)


def exchange(sections, peers, offsets, layer, probe, intensity):
    positions, extent = (intensity.shape[0], intensity.shape[-1])
    strip, columns = layer.shape[1:]
    blocks = columns // extent
    owned = positions // sections
    batch = 2 if owned % 2 == 0 else 1
    hbm = pl.BlockSpec(memory_space=pltpu.HBM)
    vmem = pl.BlockSpec(memory_space=pltpu.VMEM)
    smem = pl.BlockSpec(memory_space=pltpu.SMEM)
    tables = jnp.asarray(block_tables(extent))
    halves = (positions, 2, strip, extent)
    split_halves = (sections, owned, 2, strip, extent)
    flat, nested = (pltpu.VMEM(halves, jnp.bfloat16), pltpu.VMEM(split_halves, jnp.bfloat16))
    semaphores = pltpu.SemaphoreType.DMA((sections, owned // batch))
    return pl.pallas_call(
        functools.partial(exchange_kernel, sections, peers, batch),
        out_shape=[jax.ShapeDtypeStruct(halves, jnp.bfloat16)] * 3
        + [jax.ShapeDtypeStruct((2, positions), jnp.int32)] * 2,
        in_specs=[smem] + [hbm] * 4,
        out_specs=[vmem] * 3 + [smem] * 2,
        scratch_shapes=[
            pltpu.VMEM((blocks, 2, strip, extent), jnp.float32),
            pltpu.VMEM(probe.shape, jnp.float32),
            pltpu.VMEM((owned, extent, extent), jnp.float32),
            pltpu.VMEM((owned, extent, extent), jnp.bfloat16),
            pltpu.VMEM((owned, extent, extent), jnp.bfloat16),
            pltpu.VMEM(tables.shape, jnp.bfloat16),
            flat,
            nested,
            flat,
            flat,
            flat,
            nested,
            nested,
            nested,
            pltpu.VMEM((sections, batch, 2, extent, extent), jnp.float32),
            pltpu.VMEM((batch, 2, extent, extent), jnp.float32),
            pltpu.SemaphoreType.DMA((blocks,)),
            pltpu.SemaphoreType.DMA((3,)),
            pltpu.SemaphoreType.DMA((2,)),
            pltpu.SemaphoreType.DMA((2,)),
            pltpu.SemaphoreType.DMA((owned // batch,)),
            pltpu.SemaphoreType.DMA((owned // batch,)),
        ]
        + [semaphores] * 12,
        compiler_params=pltpu.CompilerParams(
            collective_id=0, has_side_effects=True, vmem_limit_bytes=52 * 1024 * 1024 + 192 * 1024
        ),
        name="exchange",
    )(offsets, layer, probe, intensity, tables)


def scatter_kernel(
    scan_ref, offsets_ref, near_places, far_places, own_ref, near_ref, far_ref, out_ref
):
    scan = scan_ref[0]
    positions = own_ref.shape[0]
    strip, extent = own_ref.shape[2:]
    columns = out_ref.shape[2]
    even = jnp.where(lax.rem(scan, 2) == 0, 1, 0)
    odd = 1 - even
    partner = scan + even - odd
    far = scan - even + odd
    out_ref[...] = jnp.zeros_like(out_ref)
    lanes = lax.broadcasted_iota(jnp.int32, (strip, extent), 1)

    def add(source, index, column, keep):
        first, second, shift = column_blocks(column, extent, columns)
        ahead = lanes >= shift
        for part in range(2):
            term = source[index, part].astype(jnp.float32)
            if keep is not None:
                term = jnp.where(keep, term, 0.0)
            for start, value in (
                (first, jnp.where(ahead, term, 0.0)),
                (second, jnp.where(ahead, 0.0, term)),
            ):
                place = (part, slice(None), pl.ds(start, extent))
                out_ref[place] = out_ref[place] + value

    def step(index, carry):
        add(own_ref, index, offsets_ref[1, index], None)
        near_row = near_places[0, index] - (partner - 1) * strip
        keep = kept_rows((strip, extent), near_row, even)
        add(near_ref, index, near_places[1, index], keep)
        far_row = far_places[0, index] - (far - 1) * strip
        keep = kept_rows((strip, extent), far_row, odd)
        add(far_ref, index, far_places[1, index], keep)
        return carry

    lax.fori_loop(0, positions, step, 0)


def scatter(offsets, near_places, far_places, terms, strip, columns):
    smem = pl.BlockSpec(memory_space=pltpu.SMEM)
    vmem = pl.BlockSpec(memory_space=pltpu.VMEM)
    scan = lax.axis_index("scan").astype(jnp.int32).reshape(1)
    return pl.pallas_call(
        scatter_kernel,
        out_shape=jax.ShapeDtypeStruct((2, strip, columns), jnp.float32),
        in_specs=[smem] * 4 + [vmem] * 3,
        out_specs=vmem,
        compiler_params=pltpu.CompilerParams(vmem_limit_bytes=12 * 1024 * 1024),
        name="scatter",
    )(scan, offsets, near_places, far_places, *terms)


def shards(peers, sections, object_slices, probe_wave, offsets, intensity):
    layer = object_slices[0]
    strip, columns = layer.shape[1:]
    places = offsets.T
    *terms, near_places, far_places = exchange(
        sections, peers, places, layer, probe_wave, intensity
    )
    return scatter(places, near_places, far_places, terms, strip, columns)[None]


def solution(mesh):
    in_specs = (P("depth", None, "scan", None), P(), P("scan", None), P("scan", None, None))
    out_specs = P("depth", None, "scan", None)
    body = functools.partial(shards, mesh.shape["scan"], mesh.shape["depth"])
    return jax.shard_map(body, mesh=mesh, in_specs=in_specs, out_specs=out_specs, check_vma=False)
```

```python
import functools
import math

import jax
import jax.numpy as jnp
import numpy as np
from jax import lax
from jax.experimental import pallas as pl
from jax.experimental.pallas import tpu as pltpu
from jax.sharding import PartitionSpec as P

FRESNEL = 0.0024
EARLY = 0
HALVES = (0, 1)
MESH = pl.DeviceIdType.MESH
HOP, HOP_CONJ, FOURIER, FOURIER_CONJ = range(4)
CONJUGATE_OF = {HOP: HOP_CONJ, HOP_CONJ: HOP, FOURIER: FOURIER_CONJ, FOURIER_CONJ: FOURIER}


def block_tables(extent):
    index = np.arange(extent)
    fourier = np.exp(-2j * math.pi / extent * (index[:, None] * index[None, :] % extent))
    fourier = fourier / math.sqrt(extent)
    signed = np.where(index < extent // 2, index, index - extent).astype(np.float64)
    phase = np.exp(-1j * math.pi * FRESNEL * signed * signed)
    hop = (fourier.conj() * phase[None, :]) @ fourier
    tables = []
    for matrix in (hop, hop.conj(), fourier, fourier.conj()):
        real, imag = (matrix.real, matrix.imag)
        block = np.block([[real, imag], [-imag, real]]).astype(np.float32)
        high = block.astype(jnp.bfloat16)
        tables.append(np.stack([high, (block - high.astype(np.float32)).astype(jnp.bfloat16)]))
    return np.stack(tables)


def times(first, second):
    return (
        first[0] * second[0] - first[1] * second[1],
        first[0] * second[1] + first[1] * second[0],
    )


def conj_times(first, second):
    return (
        first[0] * second[0] + first[1] * second[1],
        first[0] * second[1] - first[1] * second[0],
    )


def split(value):
    high = value.astype(jnp.bfloat16)
    return high, (value - high.astype(jnp.float32)).astype(jnp.bfloat16)


def dot(first, second):
    return jnp.dot(first, second, preferred_element_type=jnp.float32)


def right_product(fields, high, low, passes):
    extent = fields[0][0].shape[1]
    rows = [jnp.concatenate(field, axis=1) for field in fields]
    value = jnp.concatenate(rows, axis=0)
    if passes == 1:
        out = dot(value.astype(jnp.bfloat16), high)
    else:
        value_high, value_low = split(value)
        out = dot(value_high, high) + dot(value_low, high) + dot(value_high, low)
    picks = [slice(i * extent, (i + 1) * extent) for i in range(len(fields))]
    return [(out[pick, :extent], out[pick, extent:]) for pick in picks]


def left_product(fields, high, low, passes):
    extent = fields[0][0].shape[0]
    columns = [jnp.concatenate(field, axis=0) for field in fields]
    value = jnp.concatenate(columns, axis=1)
    value_high, value_low = split(value)
    if passes == 1:
        out = dot(high, value_high)
    elif len(fields) == 1:
        both = dot(high, jnp.concatenate([value_high, value_low], axis=1))
        out = both[:, :extent] + both[:, extent:] + dot(low, value_high)
    else:
        out = dot(high, value_high) + dot(high, value_low) + dot(low, value_high)
    picks = [slice(i * extent, (i + 1) * extent) for i in range(len(fields))]
    return [(out[:extent, pick], out[extent:, pick]) for pick in picks]


def transform(fields, tables_ref, kind, passes=3):
    other = CONJUGATE_OF[kind]
    fields = right_product(fields, tables_ref[kind, 0], tables_ref[kind, 1], passes)
    return left_product(fields, tables_ref[other, 0], tables_ref[other, 1], passes)


def column_blocks(column, extent, columns):
    block = column // extent
    following = jnp.minimum(block + 1, columns // extent - 1)
    first = pl.multiple_of(block * extent, extent)
    return first, pl.multiple_of(following * extent, extent), column - block * extent


def kept_rows(shape, row, above):
    inside = lax.broadcasted_iota(jnp.int32, shape, 0) >= row
    return inside.astype(jnp.int32) == above


def exchange_kernel(
    sections,
    peers,
    sizes,
    offsets_hbm,
    layer_hbm,
    probe_hbm,
    intensity_hbm,
    tables_hbm,
    own_terms,
    near_terms,
    far_terms,
    own_places,
    near_places,
    far_places,
    layer,
    probe,
    intensity,
    intensity_out,
    intensity_in,
    tables,
    own_out,
    own_in,
    relay_out,
    relay_in,
    joined,
    rim_in,
    near_first,
    far_first,
    own_back,
    rim_back,
    waves,
    adjoint,
    load_sems,
    place_send,
    place_recv,
    send_sems,
    intensity_recv,
    own_recv,
    relay_recv,
    rim_recv,
    near_recv,
    last_sems,
):
    section = lax.axis_index("depth")
    scan = lax.axis_index("scan")
    even = jnp.where(lax.rem(scan, 2) == 0, 1, 0)
    odd = 1 - even
    partner = scan + even - odd
    far = scan - even + odd
    outward = scan - 2 * even + 2 * odd
    inward = scan + 2 * even - 2 * odd
    has_outward = (outward >= 0) & (outward < peers)
    has_inward = (inward >= 0) & (inward < peers)
    blocks, _, strip, extent = layer.shape
    owned = intensity.shape[0]
    starts = [sum(sizes[:i]) for i in range(len(sizes))]
    last = len(sizes) - 1

    loads = [
        pltpu.make_async_copy(source, target, load_sems.at[i])
        for i, (source, target) in enumerate(
            (
                (probe_hbm, probe),
                (intensity_hbm.at[pl.ds(section * owned, owned)], intensity),
                (tables_hbm, tables),
                (offsets_hbm, own_places),
            )
        )
    ]

    def layer_load(block):
        columns = pl.ds(pl.multiple_of(block * extent, extent), extent)
        return pltpu.make_async_copy(
            layer_hbm.at[:, :, columns], layer.at[block], load_sems.at[4]
        )

    def start_layer(block, carry):
        layer_load(block).start()
        return carry

    loads[3].start()
    lax.fori_loop(0, blocks, start_layer, 0)
    for load in loads[:3]:
        load.start()

    barrier = pltpu.get_barrier_semaphore()

    def greet(**device):
        pl.semaphore_signal(barrier, inc=1, device_id=device, device_id_type=MESH)

    def greet_section(step, carry):
        other = lax.rem(section + step, sections)
        greet(scan=partner, depth=other)

        @pl.when(step > 0)
        def _():
            greet(depth=other)

        @pl.when(has_outward)
        def _():
            greet(scan=outward, depth=other)

        @pl.when(has_inward)
        def _():
            greet(scan=inward, depth=other)

        return carry

    lax.fori_loop(0, sections, greet_section, 0)

    @pl.when(has_outward)
    def _():
        greet(scan=far)

    @pl.when(jnp.logical_not(has_inward))
    def _():
        relay_in[...] = jnp.zeros_like(relay_in)
        far_first[...] = jnp.zeros_like(far_first)

    greeted = (
        2 * sections
        - 1
        + jnp.where(has_outward, sections + 1, 0)
        + jnp.where(has_inward, sections, 0)
    )
    loads[3].wait()
    pl.semaphore_wait(barrier, greeted)

    def remote(source, target, send, recv, device):
        return pltpu.make_async_remote_copy(
            src_ref=source,
            dst_ref=target,
            send_sem=send,
            recv_sem=recv,
            device_id=device,
            device_id_type=MESH,
        )

    near_place_copy = remote(
        own_places, near_places, place_send.at[0], place_recv.at[0], {"scan": partner}
    )
    far_place_copy = remote(
        own_places, far_places, place_send.at[1], place_recv.at[1], {"scan": far}
    )
    near_place_copy.start()

    @pl.when(has_outward)
    def _():
        far_place_copy.start()

    @pl.when(jnp.logical_not(has_outward))
    def _():
        def clear(index, carry):
            far_places[0, index] = 0
            far_places[1, index] = 0
            return carry

        lax.fori_loop(0, far_places.shape[1], clear, 0)

    def of_owner(owner, group):
        return pl.ds(owner * owned + starts[group], sizes[group])

    def of_group(group):
        return pl.ds(starts[group], sizes[group])

    def members(owner, group):
        return [
            (starts[group] + item, owner * owned + starts[group] + item)
            for item in range(sizes[group])
        ]

    def own_copy(owner, sender, group):
        return remote(
            own_out.at[of_owner(owner, group)],
            own_in.at[sender, of_group(group)],
            send_sems.at[0],
            own_recv.at[group],
            {"scan": partner, "depth": owner},
        )

    def intensity_copy(group):
        return remote(
            intensity_out.at[of_group(group)],
            intensity_in.at[of_group(group)],
            send_sems.at[1],
            intensity_recv.at[group],
            {"scan": partner},
        )

    def relay_copy(owner, group):
        return remote(
            relay_out.at[of_owner(owner, group)],
            relay_in.at[owner, of_group(group)],
            send_sems.at[2],
            relay_recv.at[group],
            {"scan": outward},
        )

    def far_first_copy(owner):
        return remote(
            relay_out.at[of_owner(owner, 0)],
            far_first.at[section],
            send_sems.at[2],
            relay_recv.at[0],
            {"scan": outward, "depth": owner},
        )

    def near_first_copy(owner):
        return remote(
            joined.at[of_owner(owner, 0)],
            near_first.at[section],
            send_sems.at[3],
            rim_recv.at[0],
            {"depth": owner},
        )

    def rim_copy(owner, sender, group):
        return remote(
            joined.at[of_owner(owner, group)],
            rim_in.at[sender, of_group(group)],
            send_sems.at[3],
            rim_recv.at[group],
            {"depth": owner},
        )

    def own_back_copy(target, sender, group):
        return remote(
            own_back.at[target, of_group(group)],
            own_terms.at[of_owner(sender, group)],
            send_sems.at[4],
            last_sems.at[0],
            {"scan": partner, "depth": target},
        )

    def rim_back_copy(target, sender, group):
        return remote(
            rim_back.at[target, of_group(group)],
            near_terms.at[sender, of_group(group)],
            send_sems.at[5],
            near_recv.at[group],
            {"depth": target},
        )

    def onward_copy(source, owner, group):
        return remote(
            source.at[owner, of_group(group)],
            far_terms.at[of_owner(owner, group)],
            send_sems.at[6],
            last_sems.at[1],
            {"scan": inward},
        )

    def far_last_copy(target):
        return remote(
            rim_back.at[target, of_group(last)],
            far_terms.at[of_owner(section, last)],
            send_sems.at[6],
            last_sems.at[1],
            {"scan": inward, "depth": target},
        )

    def keep_near(group):
        return pltpu.make_async_copy(
            rim_back.at[section, of_group(group)],
            near_terms.at[section, of_group(group)],
            last_sems.at[2],
        )

    def sent(index, ref):
        remote(ref, ref, send_sems.at[index], last_sems.at[0], {"scan": partner}).wait_send()

    def arrived(ref, sem):
        remote(ref, ref, send_sems.at[0], sem, {"scan": partner}).wait_recv()

    others = pl.ds(0, sections - 1)

    lanes = lax.broadcasted_iota(jnp.int32, (strip, extent), 1)

    def cut(column, part):
        first = column // extent
        second = jnp.minimum(first + 1, blocks - 1)
        return jnp.where(lanes >= lax.rem(column, extent), layer[first, part], layer[second, part])

    def each_owner(group, body):
        def step(index, carry):
            body(lax.rem(section + 1 + index, sections), group)
            return carry

        lax.fori_loop(0, sections, step, 0)

    loads[1].wait()

    pltpu.make_async_copy(layer, layer, load_sems.at[4]).wait()

    def send_own(owner, group):
        for _, index in members(owner, group):
            for part in range(2):
                half = cut(own_places[1, index], part).astype(jnp.bfloat16)
                own_out[index, part] = half

        own_copy(owner, section, group).start()

        @pl.when(owner == section)
        def _():
            values = intensity[of_group(group)]
            intensity_out[of_group(group)] = values.astype(jnp.bfloat16)
            intensity_copy(group).start()

    def cut_far(owner, group):
        for _, index in members(owner, group):
            row = far_places[0, index] - (far - 1) * strip
            keep = kept_rows((strip, extent), row, odd)
            for part in range(2):
                half = jnp.where(keep, cut(far_places[1, index], part), 0.0)
                relay_out[index, part] = half.astype(jnp.bfloat16)

    def send_far_first(owner, group):
        cut_far(owner, group)
        far_first_copy(owner).start()

    def send_relay(owner, group):
        cut_far(owner, group)
        relay_copy(owner, group).start()

    def send_near_first(owner, group):
        for _, index in members(owner, group):
            for part in range(2):
                half = cut(near_places[1, index], part).astype(jnp.bfloat16)
                joined[index, part] = half

        @pl.when(owner != section)
        def _():
            near_first_copy(owner).start()

        @pl.when(owner == section)
        def _():
            near_first[section] = joined[of_owner(section, 0)]

    def await_relay(group):
        @pl.when(has_inward)
        def _():
            arrived(relay_in.at[:, of_group(group)], relay_recv.at[group])

    def near_kept(index):
        row = near_places[0, index] - (partner - 1) * strip
        return kept_rows((strip, extent), row, even)

    def send_rim(owner, group):
        for place, index in members(owner, group):
            keep = near_kept(index)
            for part in range(2):
                passed = relay_in[owner, place, part].astype(jnp.float32)
                half = jnp.where(keep, cut(near_places[1, index], part), passed)
                joined[index, part] = half.astype(jnp.bfloat16)

        @pl.when(owner != section)
        def _():
            rim_copy(owner, section, group).start()

        @pl.when(owner == section)
        def _():
            rim_in[section, of_group(group)] = joined[of_owner(section, group)]

    for group in range(len(sizes)):
        each_owner(group, send_own)

    @pl.when(has_outward)
    def _():
        far_place_copy.wait()
        each_owner(0, send_far_first)
        if last > 0:
            each_owner(1, send_relay)

    near_place_copy.wait()
    each_owner(0, send_near_first)

    @pl.when(has_outward)
    def _():
        for group in range(2, len(sizes)):
            each_owner(group, send_relay)

    loads[0].wait()
    loads[2].wait()

    def join_first():
        arrived(near_first.at[others], rim_recv.at[0])

        @pl.when(has_inward)
        def _():
            arrived(far_first, relay_recv.at[0])

        def join_slice(slice_index, carry):
            for place, index in members(section, 0):
                keep = near_kept(index)
                for part in range(2):
                    here = near_first[slice_index, place, part].astype(jnp.float32)
                    passed = far_first[slice_index, place, part].astype(jnp.float32)
                    half = jnp.where(keep, here, passed)
                    rim_in[slice_index, place, part] = half.astype(jnp.bfloat16)
            return carry

        lax.fori_loop(0, sections, join_slice, 0)

    def patch(slice_index, index):
        return tuple(
            jnp.concatenate(
                [own_in[slice_index, index, part], rim_in[slice_index, index, part]], axis=0
            ).astype(jnp.float32)
            for part in range(2)
        )

    def stored(ref, *place):
        return (ref[(*place, 0)], ref[(*place, 1)])

    final = sections - 1

    def await_near(group):
        arrived(near_terms.at[others, of_group(group)], near_recv.at[group])

    def onward(owner, group):
        @pl.when(has_inward & (owner != section))
        def _():
            onward_copy(near_terms, owner, group).start()

    def run_group(group):
        items = range(sizes[group])
        mine = members(section, group)
        if group == 0:
            join_first()
        else:
            arrived(rim_in.at[others, of_group(group)], rim_recv.at[group])
        for item, (_, index) in enumerate(mine):
            down = near_places[0, index] - (partner - 2) * strip
            right = lax.rem(near_places[1, index], extent)
            for part in range(2):
                rolled = pltpu.roll(probe[part], lax.rem(down, extent), 0)
                waves[0, item, part] = pltpu.roll(rolled, right, 1)
        arrived(own_in.at[:, of_group(group)], own_recv.at[group])

        def prepare(step, joined_group):
            if joined_group is not None:

                @pl.when(step == 0)
                def _():
                    await_relay(joined_group)

                send_rim(lax.rem(section + 1 + step, sections), joined_group)

        def excite(slice_index):
            return [
                times(patch(slice_index, place), stored(waves, slice_index, item))
                for item, (place, _) in enumerate(mine)
            ]

        def forward(slice_index, inner):
            result = transform(excite(slice_index), tables, HOP)
            for item in items:
                for part in range(2):
                    waves[slice_index + 1, item, part] = result[item][part]
            prepare(slice_index, joins.get((group, 0)))
            return inner

        lax.fori_loop(0, final, forward, 0)
        fields = transform(excite(final), tables, FOURIER)
        if group > 0:
            await_near(group - 1)
            each_owner(group - 1, onward)
        prepare(final, joins.get((group, 0)))
        intensity_copy(group).wait_recv()
        driven = []
        for item, (place, _) in enumerate(mine):
            real, imag = fields[item]
            misfit = real * real + imag * imag - intensity_in[place].astype(jnp.float32)
            driven.append((misfit * real, misfit * imag))
        fields = transform(driven, tables, FOURIER_CONJ)
        for item in items:
            for part in range(2):
                adjoint[item, part] = fields[item][part]

        def give(slice_index):
            for item, (place, _) in enumerate(mine):
                term = conj_times(stored(waves, slice_index, item), stored(adjoint, item))
                for part in range(2):
                    value = term[part].astype(jnp.bfloat16)
                    own_back[slice_index, place, part] = value[:strip]
                    rim_back[slice_index, place, part] = value[strip:]

            if group == last:

                @pl.when(has_inward)
                def _():
                    far_last_copy(slice_index).start()

            @pl.when(slice_index != section)
            def _():
                rim_back_copy(slice_index, section, group).start()

            own_back_copy(slice_index, section, group).start()

            @pl.when(slice_index == section)
            def _():
                keep_near(group).start()

            if group < last:

                @pl.when(has_inward & (slice_index == section))
                def _():
                    onward_copy(rim_back, section, group).start()

        def backward(step, inner):
            slice_index = final - step
            give(slice_index)
            masked = [
                conj_times(patch(slice_index, place), stored(adjoint, item))
                for item, (place, _) in enumerate(mine)
            ]
            result = transform(masked, tables, HOP_CONJ, passes=1)
            for item in items:
                for part in range(2):
                    adjoint[item, part] = result[item][part]
            prepare(step, joins.get((group, 1)))
            return inner

        lax.fori_loop(0, final, backward, 0)
        give(0)
        prepare(final, joins.get((group, 1)))

    early = min(EARLY, last)
    for group in range(1, 1 + early):
        await_relay(group)
        each_owner(group, send_rim)
    slots = [(group, half) for group in range(len(sizes)) for half in HALVES]
    joins = dict(zip(slots, range(1 + early, len(sizes))))
    for group in range(len(sizes)):
        run_group(group)

    await_near(last)
    for index, ref in (
        (0, own_out),
        (1, intensity_out),
        (3, rim_in.at[others]),
        (4, own_back),
        (5, rim_back.at[others]),
    ):
        sent(index, ref)

    arrived(own_terms, last_sems.at[0])
    near_mine = near_terms.at[section]
    pltpu.make_async_copy(near_mine, near_mine, last_sems.at[2]).wait()

    @pl.when(has_outward)
    def _():
        sent(2, relay_out)
        arrived(far_terms, last_sems.at[1])

    @pl.when(has_inward)
    def _():
        sent(6, far_terms)


def exchange(sections, peers, offsets, layer, probe, intensity):
    positions, extent = (intensity.shape[0], intensity.shape[-1])
    strip, columns = layer.shape[1:]
    blocks = columns // extent
    owned = positions // sections
    sizes = [1] * owned
    hbm = pl.BlockSpec(memory_space=pltpu.HBM)
    smem = pl.BlockSpec(memory_space=pltpu.SMEM)
    tables = jnp.asarray(block_tables(extent))
    halves = (positions, 2, strip, extent)
    split_halves = (sections, owned, 2, strip, extent)
    flat, nested = (pltpu.VMEM(halves, jnp.bfloat16), pltpu.VMEM(split_halves, jnp.bfloat16))
    per_group = pltpu.SemaphoreType.DMA((len(sizes),))
    batch = max(sizes)
    first = pltpu.VMEM((sections, sizes[0], 2, strip, extent), jnp.bfloat16)
    out = pl.pallas_call(
        functools.partial(exchange_kernel, sections, peers, sizes),
        out_shape=[jax.ShapeDtypeStruct(x, jnp.bfloat16) for x in (halves, split_halves, halves)]
        + [jax.ShapeDtypeStruct((2, positions), jnp.int32)] * 3,
        in_specs=[hbm] * 5,
        out_specs=[hbm] * 3 + [smem] * 3,
        scratch_shapes=[
            pltpu.VMEM((blocks, 2, strip, extent), jnp.float32),
            pltpu.VMEM(probe.shape, jnp.float32),
            pltpu.VMEM((owned, extent, extent), jnp.float32),
            pltpu.VMEM((owned, extent, extent), jnp.bfloat16),
            pltpu.VMEM((owned, extent, extent), jnp.bfloat16),
            pltpu.VMEM(tables.shape, jnp.bfloat16),
            flat,
            nested,
            flat,
            nested,
            flat,
            nested,
            first,
            first,
            nested,
            nested,
            pltpu.VMEM((sections, batch, 2, extent, extent), jnp.float32),
            pltpu.VMEM((batch, 2, extent, extent), jnp.float32),
            pltpu.SemaphoreType.DMA((5,)),
            pltpu.SemaphoreType.DMA((2,)),
            pltpu.SemaphoreType.DMA((2,)),
            pltpu.SemaphoreType.DMA((7,)),
            per_group,
            per_group,
            per_group,
            per_group,
            per_group,
            pltpu.SemaphoreType.DMA((3,)),
        ],
        compiler_params=pltpu.CompilerParams(
            collective_id=0, has_side_effects=True, vmem_limit_bytes=56 * 1024 * 1024
        ),
        name="exchange",
    )(offsets, layer, probe, intensity, tables)
    return out[:3], out[3:]


def scatter_kernel(
    peers,
    own_places_hbm,
    near_places_hbm,
    far_places_hbm,
    own_hbm,
    near_hbm,
    far_hbm,
    out_hbm,
    own_places,
    near_places,
    far_places,
    own_ref,
    near_ref,
    far_ref,
    total,
    load_sems,
    store_sems,
):
    scan = lax.axis_index("scan")
    positions = own_ref.shape[0]
    strip, extent = own_ref.shape[2:]
    columns = total.shape[2]
    even = jnp.where(lax.rem(scan, 2) == 0, 1, 0)
    odd = 1 - even
    partner = scan + even - odd
    far = scan - even + odd
    has_far = (far >= 0) & (far < peers)

    loads = [
        pltpu.make_async_copy(source, target, load_sems.at[i])
        for i, (source, target) in enumerate(
            (
                (own_places_hbm, own_places),
                (near_places_hbm, near_places),
                (far_places_hbm, far_places),
                (own_hbm, own_ref),
                (near_hbm, near_ref),
                (far_hbm, far_ref),
            )
        )
    ]
    for load in loads:
        load.start()
    total[...] = jnp.zeros_like(total)
    lanes = lax.broadcasted_iota(jnp.int32, (strip, extent), 1)

    def add(part, source, index, column, keep):
        first, second, shift = column_blocks(column, extent, columns)
        ahead = lanes >= shift
        term = source[index, part].astype(jnp.float32)
        if keep is not None:
            term = jnp.where(keep, term, 0.0)
        for start, value in (
            (first, jnp.where(ahead, term, 0.0)),
            (second, jnp.where(ahead, 0.0, term)),
        ):
            place = (part, slice(None), pl.ds(start, extent))
            total[place] = total[place] + value

    def add_all(part, source, places, neighbour, above):
        def step(index, carry):
            row = places[0, index] - (neighbour - 1) * strip
            keep = None if above is None else kept_rows((strip, extent), row, above)
            add(part, source, index, places[1, index], keep)
            return carry

        lax.fori_loop(0, positions, step, 0)

    stores = []
    for part in range(2):
        if part == 0:
            loads[0].wait()
            loads[3].wait()
        add_all(part, own_ref, own_places, scan, None)
        if part == 0:
            loads[1].wait()
            loads[4].wait()
        add_all(part, near_ref, near_places, partner, even)
        if part == 0:
            loads[2].wait()
            loads[5].wait()

        @pl.when(has_far)
        def _():
            add_all(part, far_ref, far_places, far, odd)

        stores.append(
            pltpu.make_async_copy(total.at[part], out_hbm.at[part], store_sems.at[part])
        )
        stores[-1].start()
    for store in stores:
        store.wait()


def scatter(peers, places, terms, strip, columns):
    hbm = pl.BlockSpec(memory_space=pltpu.HBM)
    terms = [term.reshape(-1, *term.shape[-3:]) for term in terms]
    return pl.pallas_call(
        functools.partial(scatter_kernel, peers),
        out_shape=jax.ShapeDtypeStruct((2, strip, columns), jnp.float32),
        in_specs=[hbm] * 6,
        out_specs=hbm,
        scratch_shapes=[pltpu.SMEM(place.shape, place.dtype) for place in places]
        + [pltpu.VMEM(term.shape, term.dtype) for term in terms]
        + [
            pltpu.VMEM((2, strip, columns), jnp.float32),
            pltpu.SemaphoreType.DMA((6,)),
            pltpu.SemaphoreType.DMA((2,)),
        ],
        compiler_params=pltpu.CompilerParams(vmem_limit_bytes=56 * 1024 * 1024),
        name="scatter",
    )(*places, *terms)


def shards(peers, sections, object_slices, probe_wave, offsets, intensity):
    layer = object_slices[0]
    strip, columns = layer.shape[1:]
    places = offsets.T
    terms, taken = exchange(sections, peers, places, layer, probe_wave, intensity)
    return scatter(peers, taken, terms, strip, columns)[None]


def solution(mesh):
    in_specs = (P("depth", None, "scan", None), P(), P("scan", None), P("scan", None, None))
    out_specs = P("depth", None, "scan", None)
    body = functools.partial(shards, mesh.shape["scan"], mesh.shape["depth"])
    return jax.shard_map(body, mesh=mesh, in_specs=in_specs, out_specs=out_specs, check_vma=False)
```

```python
import functools
import math

import jax
import jax.numpy as jnp
import numpy as np
from jax import lax
from jax.experimental import pallas as pl
from jax.experimental.pallas import tpu as pltpu
from jax.sharding import PartitionSpec as P

FRESNEL = 0.0024
MESH = pl.DeviceIdType.MESH
HOP, HOP_CONJ, FOURIER, FOURIER_CONJ = range(4)
CONJUGATE_OF = {HOP: HOP_CONJ, HOP_CONJ: HOP, FOURIER: FOURIER_CONJ, FOURIER_CONJ: FOURIER}


def block_tables(extent):
    index = np.arange(extent)
    fourier = np.exp(-2j * math.pi / extent * (index[:, None] * index[None, :] % extent))
    fourier = fourier / math.sqrt(extent)
    signed = np.where(index < extent // 2, index, index - extent).astype(np.float64)
    phase = np.exp(-1j * math.pi * FRESNEL * signed * signed)
    hop = (fourier.conj() * phase[None, :]) @ fourier
    tables = []
    for matrix in (hop, hop.conj(), fourier, fourier.conj()):
        real, imag = (matrix.real, matrix.imag)
        block = np.block([[real, imag], [-imag, real]]).astype(np.float32)
        high = block.astype(jnp.bfloat16)
        tables.append(np.stack([high, (block - high.astype(np.float32)).astype(jnp.bfloat16)]))
    return np.stack(tables)


def times(first, second):
    return (
        first[0] * second[0] - first[1] * second[1],
        first[0] * second[1] + first[1] * second[0],
    )


def conj_times(first, second):
    return (
        first[0] * second[0] + first[1] * second[1],
        first[0] * second[1] - first[1] * second[0],
    )


def split(value):
    high = value.astype(jnp.bfloat16)
    return high, (value - high.astype(jnp.float32)).astype(jnp.bfloat16)


def dot(first, second):
    return jnp.dot(first, second, preferred_element_type=jnp.float32)


def right_product(fields, high, low, passes):
    extent = fields[0][0].shape[1]
    rows = [jnp.concatenate(field, axis=1) for field in fields]
    value = jnp.concatenate(rows, axis=0)
    if passes == 1:
        out = dot(value.astype(jnp.bfloat16), high)
    else:
        value_high, value_low = split(value)
        out = dot(value_high, high) + dot(value_low, high) + dot(value_high, low)
    picks = [slice(i * extent, (i + 1) * extent) for i in range(len(fields))]
    return [(out[pick, :extent], out[pick, extent:]) for pick in picks]


def left_product(fields, high, low, passes):
    extent = fields[0][0].shape[0]
    columns = [jnp.concatenate(field, axis=0) for field in fields]
    value = jnp.concatenate(columns, axis=1)
    value_high, value_low = split(value)
    if passes == 1:
        out = dot(high, value_high)
    elif len(fields) == 1:
        both = dot(high, jnp.concatenate([value_high, value_low], axis=1))
        out = both[:, :extent] + both[:, extent:] + dot(low, value_high)
    else:
        out = dot(high, value_high) + dot(high, value_low) + dot(low, value_high)
    picks = [slice(i * extent, (i + 1) * extent) for i in range(len(fields))]
    return [(out[:extent, pick], out[extent:, pick]) for pick in picks]


def transform(fields, tables_ref, kind, passes=3):
    other = CONJUGATE_OF[kind]
    fields = right_product(fields, tables_ref[kind, 0], tables_ref[kind, 1], passes)
    return left_product(fields, tables_ref[other, 0], tables_ref[other, 1], passes)


def split_column(column, extent):
    return lax.shift_right_logical(column, extent.bit_length() - 1), column & (extent - 1)


def column_blocks(column, extent, columns):
    block, shift = split_column(column, extent)
    following = jnp.minimum(block + 1, columns // extent - 1)
    first = pl.multiple_of(block * extent, extent)
    return first, pl.multiple_of(following * extent, extent), shift


def kept_rows(shape, row, above):
    inside = lax.broadcasted_iota(jnp.int32, shape, 0) >= row
    return inside.astype(jnp.int32) == above


def exchange_kernel(
    sections,
    peers,
    offsets_hbm,
    layer_hbm,
    probe_hbm,
    intensity_hbm,
    tables_hbm,
    own_terms,
    near_terms,
    far_terms,
    own_places,
    near_places,
    far_places,
    layer,
    probe,
    intensity,
    intensity_out,
    intensity_in,
    tables,
    own_out,
    own_in,
    relay_out,
    relay_in,
    joined,
    rim_in,
    near_first,
    far_first,
    own_back,
    rim_back,
    waves_even,
    waves_odd,
    adjoint_even,
    adjoint_odd,
    load_sems,
    place_send,
    place_recv,
    send_sems,
    intensity_recv,
    own_recv,
    relay_recv,
    rim_recv,
    near_recv,
    kept_sems,
    last_sems,
):
    waves, adjoint = ((waves_even, waves_odd), (adjoint_even, adjoint_odd))
    section = lax.axis_index("depth")
    scan = lax.axis_index("scan")
    even = jnp.where(lax.rem(scan, 2) == 0, 1, 0)
    odd = 1 - even
    partner = scan + even - odd
    far = scan - even + odd
    outward = scan - 2 * even + 2 * odd
    inward = scan + 2 * even - 2 * odd
    has_outward = (outward >= 0) & (outward < peers)
    has_inward = (inward >= 0) & (inward < peers)
    blocks, _, strip, extent = layer.shape
    owned = intensity.shape[0]
    last = owned - 1

    loads = [
        pltpu.make_async_copy(source, target, load_sems.at[i])
        for i, (source, target) in enumerate(
            (
                (probe_hbm, probe),
                (intensity_hbm.at[pl.ds(section * owned, owned)], intensity),
                (tables_hbm, tables),
                (offsets_hbm, own_places),
            )
        )
    ]

    def layer_load(block):
        columns = pl.ds(pl.multiple_of(block * extent, extent), extent)
        return pltpu.make_async_copy(
            layer_hbm.at[:, :, columns], layer.at[block], load_sems.at[4]
        )

    def start_layer(block, carry):
        layer_load(block).start()
        return carry

    loads[3].start()
    lax.fori_loop(0, blocks, start_layer, 0)
    for load in loads[:3]:
        load.start()

    barrier = pltpu.get_barrier_semaphore()

    def greet(**device):
        pl.semaphore_signal(barrier, inc=1, device_id=device, device_id_type=MESH)

    def greet_section(step, carry):
        other = lax.rem(section + step, sections)
        greet(scan=partner, depth=other)

        @pl.when(step > 0)
        def _():
            greet(depth=other)

        @pl.when(has_outward)
        def _():
            greet(scan=outward, depth=other)

        @pl.when(has_inward)
        def _():
            greet(scan=inward, depth=other)

        return carry

    lax.fori_loop(0, sections, greet_section, 0)

    @pl.when(has_outward)
    def _():
        greet(scan=far)

    @pl.when(jnp.logical_not(has_inward))
    def _():
        relay_in[...] = jnp.zeros_like(relay_in)
        far_first[...] = jnp.zeros_like(far_first)

    greeted = (
        2 * sections
        - 1
        + jnp.where(has_outward, sections + 1, 0)
        + jnp.where(has_inward, sections, 0)
    )
    loads[3].wait()
    pl.semaphore_wait(barrier, greeted)

    def remote(source, target, send, recv, device):
        return pltpu.make_async_remote_copy(
            src_ref=source,
            dst_ref=target,
            send_sem=send,
            recv_sem=recv,
            device_id=device,
            device_id_type=MESH,
        )

    near_place_copy = remote(
        own_places, near_places, place_send.at[0], place_recv.at[0], {"scan": partner}
    )
    far_place_copy = remote(
        own_places, far_places, place_send.at[1], place_recv.at[1], {"scan": far}
    )
    near_place_copy.start()

    @pl.when(has_outward)
    def _():
        far_place_copy.start()

    @pl.when(jnp.logical_not(has_outward))
    def _():
        def clear(index, carry):
            far_places[0, index] = 0
            far_places[1, index] = 0
            return carry

        lax.fori_loop(0, far_places.shape[1], clear, 0)

    def own_copy(owner, sender, first, count):
        return remote(
            own_out.at[owner, pl.ds(first, count)],
            own_in.at[sender, pl.ds(first, count)],
            send_sems.at[0],
            own_recv.at[first],
            {"scan": partner, "depth": owner},
        )

    def intensity_copy(first, count):
        return remote(
            intensity_out.at[pl.ds(first, count)],
            intensity_in.at[pl.ds(first, count)],
            send_sems.at[1],
            intensity_recv.at[first],
            {"scan": partner},
        )

    def relay_copy(place):
        return remote(
            relay_out.at[place],
            relay_in.at[place],
            send_sems.at[2],
            relay_recv.at[place],
            {"scan": outward},
        )

    def far_first_copy(owner):
        return remote(
            relay_out.at[0, owner],
            far_first.at[section],
            send_sems.at[2],
            relay_recv.at[0],
            {"scan": outward, "depth": owner},
        )

    def near_first_copy(owner):
        return remote(
            joined.at[0, owner],
            near_first.at[section],
            send_sems.at[3],
            rim_recv.at[0],
            {"depth": owner},
        )

    def rim_copy(owner, place):
        return remote(
            joined.at[place, owner],
            rim_in.at[place, section],
            send_sems.at[3],
            rim_recv.at[place],
            {"depth": owner},
        )

    def own_back_copy(target, place):
        return remote(
            own_back.at[place, target],
            own_terms.at[place, section],
            send_sems.at[4],
            last_sems.at[0],
            {"scan": partner, "depth": target},
        )

    def rim_back_copy(target, place):
        return remote(
            rim_back.at[place, target],
            near_terms.at[place, section],
            send_sems.at[5],
            near_recv.at[place],
            {"depth": target},
        )

    def keep_near(place):
        return pltpu.make_async_copy(
            rim_back.at[place, section], near_terms.at[place, section], kept_sems.at[place]
        )

    def onward_copy(place):
        return remote(
            near_terms.at[place],
            far_terms.at[place],
            send_sems.at[6],
            last_sems.at[1],
            {"scan": inward},
        )

    def far_last_copy(target):
        return remote(
            rim_back.at[last, target],
            far_terms.at[last, section],
            send_sems.at[6],
            last_sems.at[1],
            {"scan": inward, "depth": target},
        )

    def sent(index, ref):
        remote(ref, ref, send_sems.at[index], last_sems.at[0], {"scan": partner}).wait_send()

    def arrived(ref, sem):
        remote(ref, ref, send_sems.at[0], sem, {"scan": partner}).wait_recv()

    others = pl.ds(0, sections - 1)

    lanes = lax.broadcasted_iota(jnp.int32, (strip, extent), 1)

    def cut(column):
        first, shift = split_column(column, extent)
        second = jnp.minimum(first + 1, blocks - 1)
        ahead = lanes >= shift
        return [jnp.where(ahead, layer[first, part], layer[second, part]) for part in range(2)]

    order = [lax.rem(section + 1 + step, sections) for step in range(sections)]

    loads[1].wait()

    pltpu.make_async_copy(layer, layer, load_sems.at[4]).wait()

    def cut_own(place):
        for owner in order:
            for part, half in enumerate(cut(own_places[1, owner * owned + place])):
                own_out[owner, place, part] = half.astype(jnp.bfloat16)

    def send_own(first, count):
        lax.fori_loop(first, first + count, lambda place, carry: (cut_own(place), carry)[1], 0)
        for owner in order:
            own_copy(owner, section, first, count).start()

    def send_intensity(first, count):
        picked = pl.ds(first, count)
        intensity_out[picked] = intensity[picked].astype(jnp.bfloat16)
        intensity_copy(first, count).start()

    def cut_far(place):
        for owner in order:
            index = owner * owned + place
            keep = kept_rows((strip, extent), far_places[0, index] - (far - 1) * strip, odd)
            for part, half in enumerate(cut(far_places[1, index])):
                relay_out[place, owner, part] = jnp.where(keep, half, 0.0).astype(jnp.bfloat16)

    def send_relay(place, carry):
        cut_far(place)
        relay_copy(place).start()
        return carry

    def near_kept(index):
        row = near_places[0, index] - (partner - 1) * strip
        return kept_rows((strip, extent), row, even)

    def send_near_first():
        for owner in order:
            for part, half in enumerate(cut(near_places[1, owner * owned])):
                joined[0, owner, part] = half.astype(jnp.bfloat16)
        near_first[section] = joined[0, section]
        for owner in order[:-1]:
            near_first_copy(owner).start()

    def await_relay(place):
        @pl.when(has_inward)
        def _():
            arrived(relay_in.at[place], relay_recv.at[place])

    def send_rim(owner, place):
        index = owner * owned + place
        keep = near_kept(index)
        for part, half in enumerate(cut(near_places[1, index])):
            passed = relay_in[place, owner, part].astype(jnp.float32)
            joined[place, owner, part] = jnp.where(keep, half, passed).astype(jnp.bfloat16)

        @pl.when(owner != section)
        def _():
            rim_copy(owner, place).start()

        @pl.when(owner == section)
        def _():
            rim_in[place, section] = joined[place, section]

    chunks = [(first, 1) for first in range(min(owned, 2))]
    if owned > 2:
        chunks.append((2, owned - 2))
    for first, count in chunks:
        send_own(first, count)
        send_intensity(first, count)

    @pl.when(has_outward)
    def _():
        far_place_copy.wait()
        cut_far(0)
        for owner in order:
            far_first_copy(owner).start()

    near_place_copy.wait()
    send_near_first()

    @pl.when(has_outward)
    def _():
        lax.fori_loop(1, owned, send_relay, 0)

    loads[0].wait()
    loads[2].wait()

    def join_first():
        arrived(near_first.at[others], rim_recv.at[0])

        @pl.when(has_inward)
        def _():
            arrived(far_first, relay_recv.at[0])

        keep = near_kept(section * owned)

        def join_slice(slice_index, carry):
            for part in range(2):
                here = near_first[slice_index, part].astype(jnp.float32)
                passed = far_first[slice_index, part].astype(jnp.float32)
                rim_in[0, slice_index, part] = jnp.where(keep, here, passed).astype(jnp.bfloat16)
            return carry

        lax.fori_loop(0, sections, join_slice, 0)

    def patch(slice_index, place):
        return tuple(
            jnp.concatenate(
                [own_in[slice_index, place, part], rim_in[place, slice_index, part]], axis=0
            ).astype(jnp.float32)
            for part in range(2)
        )

    def stored(ref, *place):
        return (ref[(*place, 0)], ref[(*place, 1)])

    def store(ref, place, field):
        for part in range(2):
            ref[(*place, part)] = field[part]

    final = sections - 1

    def await_near(place):
        arrived(near_terms.at[place, others], near_recv.at[place])
        keep_near(place).wait()

    def prepare(step, place):
        if place is not None:
            if isinstance(step, int):
                if step == 0:
                    await_relay(place)
            else:
                pl.when(step == 0)(lambda: await_relay(place))

            send_rim(lax.rem(section + 1 + step, sections), place)

    def begin(place):
        if place == 0:
            join_first()
        else:
            arrived(rim_in.at[place, others], rim_recv.at[place])
        index = section * owned + place
        down = near_places[0, index] - (partner - 2) * strip
        right = lax.rem(near_places[1, index], extent)
        rolled = [pltpu.roll(probe[part], lax.rem(down, extent), 0) for part in range(2)]
        store(waves[place % 2], (0,), [pltpu.roll(value, right, 1) for value in rolled])
        for first, count in chunks:
            if first == place:
                arrived(own_in.at[:, pl.ds(first, count)], own_recv.at[first])

    def excite(place, slice_index):
        return times(patch(slice_index, place), stored(waves[place % 2], slice_index))

    def forward(place, slice_index):
        return transform([excite(place, slice_index)], tables, HOP)[0]

    def turn(place):
        (real, imag), = transform([excite(place, final)], tables, FOURIER)
        for first, count in chunks:
            if first == place:
                intensity_copy(first, count).wait_recv()
        misfit = real * real + imag * imag - intensity_in[place].astype(jnp.float32)
        driven = (misfit * real, misfit * imag)
        store(adjoint[place % 2], (), transform([driven], tables, FOURIER_CONJ)[0])

    def give(place, slice_index):
        term = conj_times(stored(waves[place % 2], slice_index), stored(adjoint[place % 2]))
        for part in range(2):
            value = term[part].astype(jnp.bfloat16)
            own_back[place, slice_index, part] = value[:strip]
            rim_back[place, slice_index, part] = value[strip:]

        if place == last:

            @pl.when(has_inward)
            def _():
                far_last_copy(slice_index).start()

        @pl.when(slice_index != section)
        def _():
            rim_back_copy(slice_index, place).start()

        @pl.when(slice_index == section)
        def _():
            keep_near(place).start()

        own_back_copy(slice_index, place).start()

    def backward(place, slice_index):
        masked = conj_times(patch(slice_index, place), stored(adjoint[place % 2]))
        return transform([masked], tables, HOP_CONJ, passes=1)[0]

    def run_position(place, early, late):
        begin(place)

        def forward_step(index, carry):
            store(waves[place % 2], (index + 1,), forward(place, index))
            return carry

        lax.fori_loop(0, final, forward_step, 0)
        for index in range(sections):
            prepare(index, early)
        turn(place)

        def backward_step(index, carry):
            give(place, final - index)
            store(adjoint[place % 2], (), backward(place, final - index))
            prepare(index, late)
            return carry

        lax.fori_loop(0, final, backward_step, 0)
        give(place, 0)
        if place > 0:
            await_near(place - 1)

            @pl.when(has_inward)
            def _():
                onward_copy(place - 1).start()

        prepare(final, late)

    joins = [*range(1, owned), *[None] * (owned + 1)]
    for place in range(owned):
        run_position(place, *joins[2 * place : 2 * place + 2])

    await_near(last)
    for index, ref in (
        (0, own_out),
        (1, intensity_out),
        (3, joined.at[:, others]),
        (4, own_back),
        (5, rim_back.at[:, others]),
    ):
        sent(index, ref)

    arrived(own_terms, last_sems.at[0])

    @pl.when(has_outward)
    def _():
        sent(2, relay_out)
        arrived(far_terms, last_sems.at[1])

    @pl.when(has_inward)
    def _():
        sent(6, far_terms)


def exchange(sections, peers, offsets, layer, probe, intensity):
    positions, extent = (intensity.shape[0], intensity.shape[-1])
    strip, columns = layer.shape[1:]
    blocks = columns // extent
    owned = positions // sections
    hbm = pl.BlockSpec(memory_space=pltpu.HBM)
    smem = pl.BlockSpec(memory_space=pltpu.SMEM)
    tables = jnp.asarray(block_tables(extent))
    by_place = (owned, sections, 2, strip, extent)
    by_owner = (sections, owned, 2, strip, extent)
    first = (sections, 2, strip, extent)
    buffers = (by_owner, by_owner, by_place, by_place, by_place, by_place, first, first)
    buffers += (by_place, by_place)
    per_place = pltpu.SemaphoreType.DMA((owned,))
    out = pl.pallas_call(
        functools.partial(exchange_kernel, sections, peers),
        out_shape=[jax.ShapeDtypeStruct(by_place, jnp.bfloat16)] * 3
        + [jax.ShapeDtypeStruct((2, positions), jnp.int32)] * 3,
        in_specs=[hbm] * 5,
        out_specs=[hbm] * 3 + [smem] * 3,
        scratch_shapes=[
            pltpu.VMEM((blocks, 2, strip, extent), jnp.float32),
            pltpu.VMEM(probe.shape, jnp.float32),
            pltpu.VMEM((owned, extent, extent), jnp.float32),
            pltpu.VMEM((owned, extent, extent), jnp.bfloat16),
            pltpu.VMEM((owned, extent, extent), jnp.bfloat16),
            pltpu.VMEM(tables.shape, jnp.bfloat16),
            *[pltpu.VMEM(shape, jnp.bfloat16) for shape in buffers],
            *[pltpu.VMEM((sections, 2, extent, extent), jnp.float32)] * 2,
            *[pltpu.VMEM((2, extent, extent), jnp.float32)] * 2,
            pltpu.SemaphoreType.DMA((5,)),
            pltpu.SemaphoreType.DMA((2,)),
            pltpu.SemaphoreType.DMA((2,)),
            pltpu.SemaphoreType.DMA((7,)),
            *[per_place] * 6,
            pltpu.SemaphoreType.DMA((2,)),
        ],
        compiler_params=pltpu.CompilerParams(
            collective_id=0, has_side_effects=True, vmem_limit_bytes=56 * 1024 * 1024
        ),
        name="exchange",
    )(offsets, layer, probe, intensity, tables)
    return out[:3], out[3:]


def scatter_kernel(
    peers,
    sections,
    own_places_hbm,
    near_places_hbm,
    far_places_hbm,
    own_hbm,
    near_hbm,
    far_hbm,
    out_hbm,
    own_places,
    near_places,
    far_places,
    own_ref,
    near_ref,
    far_ref,
    total,
    load_sems,
    store_sems,
):
    scan = lax.axis_index("scan")
    positions = own_ref.shape[0]
    strip, extent = own_ref.shape[2:]
    columns = total.shape[2]
    even = jnp.where(lax.rem(scan, 2) == 0, 1, 0)
    odd = 1 - even
    partner = scan + even - odd
    far = scan - even + odd
    has_far = (far >= 0) & (far < peers)

    loads = [
        pltpu.make_async_copy(source, target, load_sems.at[i])
        for i, (source, target) in enumerate(
            (
                (own_places_hbm, own_places),
                (near_places_hbm, near_places),
                (far_places_hbm, far_places),
                (own_hbm, own_ref),
                (near_hbm, near_ref),
                (far_hbm, far_ref),
            )
        )
    ]
    for load in loads:
        load.start()
    total[...] = jnp.zeros_like(total)
    lanes = lax.broadcasted_iota(jnp.int32, (strip, extent), 1)

    def add(part, source, index, column, keep):
        first, second, shift = column_blocks(column, extent, columns)
        ahead = lanes >= shift
        term = source[index, part].astype(jnp.float32)
        if keep is not None:
            term = jnp.where(keep, term, 0.0)
        for start, value in (
            (first, jnp.where(ahead, term, 0.0)),
            (second, jnp.where(ahead, 0.0, term)),
        ):
            place = (part, slice(None), pl.ds(start, extent))
            total[place] = total[place] + value

    def add_all(part, source, places, neighbour, above):
        def step(index, carry):
            owner, place = (lax.rem(index, sections), lax.div(index, sections))
            position = owner * (positions // sections) + place
            row = places[0, position] - (neighbour - 1) * strip
            keep = None if above is None else kept_rows((strip, extent), row, above)
            add(part, source, index, places[1, position], keep)
            return carry

        lax.fori_loop(0, positions, step, 0)

    stores = []
    for part in range(2):
        if part == 0:
            loads[0].wait()
            loads[3].wait()
        add_all(part, own_ref, own_places, scan, None)
        if part == 0:
            loads[1].wait()
            loads[4].wait()
        add_all(part, near_ref, near_places, partner, even)
        if part == 0:
            loads[2].wait()
            loads[5].wait()

        @pl.when(has_far)
        def _():
            add_all(part, far_ref, far_places, far, odd)

        stores.append(
            pltpu.make_async_copy(total.at[part], out_hbm.at[part], store_sems.at[part])
        )
        stores[-1].start()
    for store in stores:
        store.wait()


def scatter(peers, sections, places, terms, strip, columns):
    hbm = pl.BlockSpec(memory_space=pltpu.HBM)
    terms = [term.reshape(-1, *term.shape[-3:]) for term in terms]
    return pl.pallas_call(
        functools.partial(scatter_kernel, peers, sections),
        out_shape=jax.ShapeDtypeStruct((2, strip, columns), jnp.float32),
        in_specs=[hbm] * 6,
        out_specs=hbm,
        scratch_shapes=[pltpu.SMEM(place.shape, place.dtype) for place in places]
        + [pltpu.VMEM(term.shape, term.dtype) for term in terms]
        + [
            pltpu.VMEM((2, strip, columns), jnp.float32),
            pltpu.SemaphoreType.DMA((6,)),
            pltpu.SemaphoreType.DMA((2,)),
        ],
        compiler_params=pltpu.CompilerParams(vmem_limit_bytes=56 * 1024 * 1024),
        name="scatter",
    )(*places, *terms)


def shards(peers, sections, object_slices, probe_wave, offsets, intensity):
    layer = object_slices[0]
    strip, columns = layer.shape[1:]
    places = offsets.T
    terms, taken = exchange(sections, peers, places, layer, probe_wave, intensity)
    return scatter(peers, sections, taken, terms, strip, columns)[None]


def solution(mesh):
    in_specs = (P("depth", None, "scan", None), P(), P("scan", None), P("scan", None, None))
    out_specs = P("depth", None, "scan", None)
    body = functools.partial(shards, mesh.shape["scan"], mesh.shape["depth"])
    return jax.shard_map(body, mesh=mesh, in_specs=in_specs, out_specs=out_specs, check_vma=False)
```

```python
import functools
import math

import jax
import jax.numpy as jnp
import numpy as np
from jax import lax
from jax.experimental import pallas as pl
from jax.experimental.pallas import tpu as pltpu
from jax.sharding import PartitionSpec as P

FRESNEL = 0.0024
MESH = pl.DeviceIdType.MESH
HOP, HOP_CONJ, FOURIER, FOURIER_CONJ = range(4)
CONJUGATE_OF = {HOP: HOP_CONJ, HOP_CONJ: HOP, FOURIER: FOURIER_CONJ, FOURIER_CONJ: FOURIER}


def block_tables(extent):
    index = np.arange(extent)
    fourier = np.exp(-2j * math.pi / extent * (index[:, None] * index[None, :] % extent))
    fourier = fourier / math.sqrt(extent)
    signed = np.where(index < extent // 2, index, index - extent).astype(np.float64)
    phase = np.exp(-1j * math.pi * FRESNEL * signed * signed)
    hop = (fourier.conj() * phase[None, :]) @ fourier
    tables = []
    for matrix in (hop, hop.conj(), fourier, fourier.conj()):
        real, imag = (matrix.real, matrix.imag)
        block = np.block([[real, imag], [-imag, real]]).astype(np.float32)
        high = block.astype(jnp.bfloat16)
        tables.append(np.stack([high, (block - high.astype(np.float32)).astype(jnp.bfloat16)]))
    return np.stack(tables)


def times(first, second):
    return (
        first[0] * second[0] - first[1] * second[1],
        first[0] * second[1] + first[1] * second[0],
    )


def conj_times(first, second):
    return (
        first[0] * second[0] + first[1] * second[1],
        first[0] * second[1] - first[1] * second[0],
    )


def split(value):
    high = value.astype(jnp.bfloat16)
    return high, (value - high.astype(jnp.float32)).astype(jnp.bfloat16)


def dot(first, second):
    return jnp.dot(first, second, preferred_element_type=jnp.float32)


def right_product(fields, high, low, passes):
    extent = fields[0][0].shape[1]
    rows = [jnp.concatenate(field, axis=1) for field in fields]
    value = jnp.concatenate(rows, axis=0)
    if passes == 1:
        out = dot(value.astype(jnp.bfloat16), high)
    else:
        value_high, value_low = split(value)
        out = dot(value_high, high) + dot(value_low, high) + dot(value_high, low)
    picks = [slice(i * extent, (i + 1) * extent) for i in range(len(fields))]
    return [(out[pick, :extent], out[pick, extent:]) for pick in picks]


def left_product(fields, high, low, passes):
    extent = fields[0][0].shape[0]
    columns = [jnp.concatenate(field, axis=0) for field in fields]
    value = jnp.concatenate(columns, axis=1)
    value_high, value_low = split(value)
    if passes == 1:
        out = dot(high, value_high)
    elif len(fields) == 1:
        both = dot(high, jnp.concatenate([value_high, value_low], axis=1))
        out = both[:, :extent] + both[:, extent:] + dot(low, value_high)
    else:
        out = dot(high, value_high) + dot(high, value_low) + dot(low, value_high)
    picks = [slice(i * extent, (i + 1) * extent) for i in range(len(fields))]
    return [(out[:extent, pick], out[extent:, pick]) for pick in picks]


def transform(fields, tables_ref, kind, passes=3):
    other = CONJUGATE_OF[kind]
    fields = right_product(fields, tables_ref[kind, 0], tables_ref[kind, 1], passes)
    return left_product(fields, tables_ref[other, 0], tables_ref[other, 1], passes)


def split_column(column, extent):
    return lax.shift_right_logical(column, extent.bit_length() - 1), column & (extent - 1)


def column_blocks(column, extent, columns):
    block, shift = split_column(column, extent)
    following = jnp.minimum(block + 1, columns // extent - 1)
    first = pl.multiple_of(block * extent, extent)
    return first, pl.multiple_of(following * extent, extent), shift


def kept_rows(shape, row, above):
    inside = lax.broadcasted_iota(jnp.int32, shape, 0) >= row
    return inside.astype(jnp.int32) == above


def exchange_kernel(
    sections,
    peers,
    offsets_hbm,
    layer_hbm,
    probe_hbm,
    intensity_hbm,
    tables_hbm,
    own_terms,
    near_terms,
    far_terms,
    own_places,
    near_places,
    far_places,
    layer,
    probe,
    intensity,
    intensity_out,
    intensity_in,
    tables,
    own_out,
    own_in,
    relay_out,
    relay_in,
    joined,
    rim_in,
    near_first,
    far_first,
    own_back,
    rim_back,
    waves_even,
    waves_odd,
    adjoint_even,
    adjoint_odd,
    load_sems,
    place_send,
    place_recv,
    send_sems,
    intensity_recv,
    own_recv,
    relay_recv,
    rim_recv,
    near_recv,
    kept_sems,
    last_sems,
):
    waves, adjoint = ((waves_even, waves_odd), (adjoint_even, adjoint_odd))
    section = lax.axis_index("depth")
    scan = lax.axis_index("scan")
    even = jnp.where(lax.rem(scan, 2) == 0, 1, 0)
    odd = 1 - even
    partner = scan + even - odd
    far = scan - even + odd
    outward = scan - 2 * even + 2 * odd
    inward = scan + 2 * even - 2 * odd
    has_outward = (outward >= 0) & (outward < peers)
    has_inward = (inward >= 0) & (inward < peers)
    blocks, _, strip, extent = layer.shape
    owned = intensity.shape[0]
    last = owned - 1
    straight = max(0, owned - 2)

    loads = [
        pltpu.make_async_copy(source, target, load_sems.at[i])
        for i, (source, target) in enumerate(
            (
                (probe_hbm, probe),
                (intensity_hbm.at[pl.ds(section * owned, owned)], intensity),
                (tables_hbm, tables),
                (offsets_hbm, own_places),
            )
        )
    ]

    def layer_load(block):
        columns = pl.ds(pl.multiple_of(block * extent, extent), extent)
        return pltpu.make_async_copy(
            layer_hbm.at[:, :, columns], layer.at[block], load_sems.at[4]
        )

    def start_layer(block, carry):
        layer_load(block).start()
        return carry

    loads[3].start()
    lax.fori_loop(0, blocks, start_layer, 0)
    for load in loads[:3]:
        load.start()

    barrier = pltpu.get_barrier_semaphore()

    def greet(**device):
        pl.semaphore_signal(barrier, inc=1, device_id=device, device_id_type=MESH)

    def greet_section(step, carry):
        other = lax.rem(section + step, sections)
        greet(scan=partner, depth=other)

        @pl.when(step > 0)
        def _():
            greet(depth=other)

        @pl.when(has_outward)
        def _():
            greet(scan=outward, depth=other)

        @pl.when(has_inward)
        def _():
            greet(scan=inward, depth=other)

        return carry

    lax.fori_loop(0, sections, greet_section, 0)

    @pl.when(has_outward)
    def _():
        greet(scan=far)

    @pl.when(jnp.logical_not(has_inward))
    def _():
        relay_in[...] = jnp.zeros_like(relay_in)
        far_first[...] = jnp.zeros_like(far_first)

    greeted = (
        2 * sections
        - 1
        + jnp.where(has_outward, sections + 1, 0)
        + jnp.where(has_inward, sections, 0)
    )
    loads[3].wait()
    pl.semaphore_wait(barrier, greeted)

    def remote(source, target, send, recv, device):
        return pltpu.make_async_remote_copy(
            src_ref=source,
            dst_ref=target,
            send_sem=send,
            recv_sem=recv,
            device_id=device,
            device_id_type=MESH,
        )

    near_place_copy = remote(
        own_places, near_places, place_send.at[0], place_recv.at[0], {"scan": partner}
    )
    far_place_copy = remote(
        own_places, far_places, place_send.at[1], place_recv.at[1], {"scan": far}
    )
    near_place_copy.start()

    @pl.when(has_outward)
    def _():
        far_place_copy.start()

    @pl.when(jnp.logical_not(has_outward))
    def _():
        def clear(index, carry):
            far_places[0, index] = 0
            far_places[1, index] = 0
            return carry

        lax.fori_loop(0, far_places.shape[1], clear, 0)

    def own_copy(owner, sender, first, count):
        return remote(
            own_out.at[owner, pl.ds(first, count)],
            own_in.at[sender, pl.ds(first, count)],
            send_sems.at[0],
            own_recv.at[first],
            {"scan": partner, "depth": owner},
        )

    def intensity_copy(first, count):
        return remote(
            intensity_out.at[pl.ds(first, count)],
            intensity_in.at[pl.ds(first, count)],
            send_sems.at[1],
            intensity_recv.at[first],
            {"scan": partner},
        )

    def relay_copy(place):
        return remote(
            relay_out.at[place],
            relay_in.at[place],
            send_sems.at[2],
            relay_recv.at[place],
            {"scan": outward},
        )

    def far_first_copy(owner):
        return remote(
            relay_out.at[0, owner],
            far_first.at[section],
            send_sems.at[2],
            relay_recv.at[0],
            {"scan": outward, "depth": owner},
        )

    def near_first_copy(owner):
        return remote(
            joined.at[0, owner],
            near_first.at[section],
            send_sems.at[3],
            rim_recv.at[0],
            {"depth": owner},
        )

    def rim_copy(owner, place):
        return remote(
            joined.at[place, owner],
            rim_in.at[place, section],
            send_sems.at[3],
            rim_recv.at[place],
            {"depth": owner},
        )

    def own_back_copy(target, place):
        return remote(
            own_back.at[place, target],
            own_terms.at[place, section],
            send_sems.at[4],
            last_sems.at[0],
            {"scan": partner, "depth": target},
        )

    def rim_back_copy(target, place):
        return remote(
            rim_back.at[place, target],
            near_terms.at[place, section],
            send_sems.at[5],
            near_recv.at[place],
            {"depth": target},
        )

    def keep_near(place):
        return pltpu.make_async_copy(
            rim_back.at[place, section], near_terms.at[place, section], kept_sems.at[place]
        )

    def onward_copy(place):
        return remote(
            near_terms.at[place],
            far_terms.at[place],
            send_sems.at[6],
            last_sems.at[1],
            {"scan": inward},
        )

    def far_last_copy(target, place):
        return remote(
            rim_back.at[place, target],
            far_terms.at[place, section],
            send_sems.at[6],
            last_sems.at[1],
            {"scan": inward, "depth": target},
        )

    def sent(index, ref):
        remote(ref, ref, send_sems.at[index], last_sems.at[0], {"scan": partner}).wait_send()

    def arrived(ref, sem):
        remote(ref, ref, send_sems.at[0], sem, {"scan": partner}).wait_recv()

    others = pl.ds(0, sections - 1)

    lanes = lax.broadcasted_iota(jnp.int32, (strip, extent), 1)

    def cut(column):
        first, shift = split_column(column, extent)
        second = jnp.minimum(first + 1, blocks - 1)
        ahead = lanes >= shift
        return [jnp.where(ahead, layer[first, part], layer[second, part]) for part in range(2)]

    order = [lax.rem(section + 1 + step, sections) for step in range(sections)]

    loads[1].wait()

    pltpu.make_async_copy(layer, layer, load_sems.at[4]).wait()

    def cut_own(place):
        for owner in order:
            for part, half in enumerate(cut(own_places[1, owner * owned + place])):
                own_out[owner, place, part] = half.astype(jnp.bfloat16)

    def send_own(first, count):
        lax.fori_loop(first, first + count, lambda place, carry: (cut_own(place), carry)[1], 0)
        for owner in order:
            own_copy(owner, section, first, count).start()

    def send_intensity(first, count):
        picked = pl.ds(first, count)
        intensity_out[picked] = intensity[picked].astype(jnp.bfloat16)
        intensity_copy(first, count).start()

    def cut_far(place):
        for owner in order:
            index = owner * owned + place
            keep = kept_rows((strip, extent), far_places[0, index] - (far - 1) * strip, odd)
            for part, half in enumerate(cut(far_places[1, index])):
                relay_out[place, owner, part] = jnp.where(keep, half, 0.0).astype(jnp.bfloat16)

    def send_relay(place, carry):
        cut_far(place)
        relay_copy(place).start()
        return carry

    def near_kept(index):
        row = near_places[0, index] - (partner - 1) * strip
        return kept_rows((strip, extent), row, even)

    def send_near_first():
        for owner in order:
            for part, half in enumerate(cut(near_places[1, owner * owned])):
                joined[0, owner, part] = half.astype(jnp.bfloat16)
        near_first[section] = joined[0, section]
        for owner in order[:-1]:
            near_first_copy(owner).start()

    def await_relay(place):
        @pl.when(has_inward)
        def _():
            arrived(relay_in.at[place], relay_recv.at[place])

    def send_rim(owner, place):
        index = owner * owned + place
        keep = near_kept(index)
        for part, half in enumerate(cut(near_places[1, index])):
            passed = relay_in[place, owner, part].astype(jnp.float32)
            joined[place, owner, part] = jnp.where(keep, half, passed).astype(jnp.bfloat16)

        @pl.when(owner != section)
        def _():
            rim_copy(owner, place).start()

        @pl.when(owner == section)
        def _():
            rim_in[place, section] = joined[place, section]

    chunks = [(first, 1) for first in range(min(owned, 2))]
    if owned > 2:
        chunks.append((2, owned - 2))
    for first, count in chunks:
        send_own(first, count)
        send_intensity(first, count)

    @pl.when(has_outward)
    def _():
        far_place_copy.wait()
        cut_far(0)
        for owner in order:
            far_first_copy(owner).start()

    near_place_copy.wait()
    send_near_first()

    @pl.when(has_outward)
    def _():
        lax.fori_loop(1, owned, send_relay, 0)

    loads[0].wait()
    loads[2].wait()

    def join_first():
        arrived(near_first.at[others], rim_recv.at[0])

        @pl.when(has_inward)
        def _():
            arrived(far_first, relay_recv.at[0])

        keep = near_kept(section * owned)

        def join_slice(slice_index, carry):
            for part in range(2):
                here = near_first[slice_index, part].astype(jnp.float32)
                passed = far_first[slice_index, part].astype(jnp.float32)
                rim_in[0, slice_index, part] = jnp.where(keep, here, passed).astype(jnp.bfloat16)
            return carry

        lax.fori_loop(0, sections, join_slice, 0)

    def patch(slice_index, place):
        return tuple(
            jnp.concatenate(
                [own_in[slice_index, place, part], rim_in[place, slice_index, part]], axis=0
            ).astype(jnp.float32)
            for part in range(2)
        )

    def stored(ref, *place):
        return (ref[(*place, 0)], ref[(*place, 1)])

    def store(ref, place, field):
        for part in range(2):
            ref[(*place, part)] = field[part]

    final = sections - 1

    def await_near(place):
        arrived(near_terms.at[place, others], near_recv.at[place])
        keep_near(place).wait()

    def prepare(step, place):
        if place is not None:
            if isinstance(step, int):
                if step == 0:
                    await_relay(place)
            else:
                pl.when(step == 0)(lambda: await_relay(place))

            send_rim(lax.rem(section + 1 + step, sections), place)

    def begin(place):
        if place == 0:
            join_first()
        else:
            arrived(rim_in.at[place, others], rim_recv.at[place])
        index = section * owned + place
        down = near_places[0, index] - (partner - 2) * strip
        right = lax.rem(near_places[1, index], extent)
        rolled = [pltpu.roll(probe[part], lax.rem(down, extent), 0) for part in range(2)]
        store(waves[place % 2], (0,), [pltpu.roll(value, right, 1) for value in rolled])
        for first, count in chunks:
            if first == place:
                arrived(own_in.at[:, pl.ds(first, count)], own_recv.at[first])

    def excite(place, slice_index):
        return times(patch(slice_index, place), stored(waves[place % 2], slice_index))

    def forward(place, slice_index):
        return transform([excite(place, slice_index)], tables, HOP)[0]

    def turn(place):
        (real, imag), = transform([excite(place, final)], tables, FOURIER)
        for first, count in chunks:
            if first == place:
                intensity_copy(first, count).wait_recv()
        misfit = real * real + imag * imag - intensity_in[place].astype(jnp.float32)
        driven = (misfit * real, misfit * imag)
        store(adjoint[place % 2], (), transform([driven], tables, FOURIER_CONJ)[0])

    def give(place, slice_index):
        term = conj_times(stored(waves[place % 2], slice_index), stored(adjoint[place % 2]))
        for part in range(2):
            value = term[part].astype(jnp.bfloat16)
            own_back[place, slice_index, part] = value[:strip]
            rim_back[place, slice_index, part] = value[strip:]

        if place >= straight:

            @pl.when(has_inward)
            def _():
                far_last_copy(slice_index, place).start()

        @pl.when(slice_index != section)
        def _():
            rim_back_copy(slice_index, place).start()

        @pl.when(slice_index == section)
        def _():
            keep_near(place).start()

        own_back_copy(slice_index, place).start()

    def backward(place, slice_index):
        masked = conj_times(patch(slice_index, place), stored(adjoint[place % 2]))
        return transform([masked], tables, HOP_CONJ, passes=1)[0]

    def run_position(place, early, late):
        begin(place)

        def forward_step(index, carry):
            store(waves[place % 2], (index + 1,), forward(place, index))
            return carry

        lax.fori_loop(0, final, forward_step, 0)
        for index in range(sections):
            prepare(index, early)
        turn(place)

        def backward_step(index, carry):
            give(place, final - index)
            store(adjoint[place % 2], (), backward(place, final - index))
            prepare(index, late)
            return carry

        lax.fori_loop(0, final, backward_step, 0)
        give(place, 0)
        if 0 < place <= straight:
            await_near(place - 1)

            @pl.when(has_inward)
            def _():
                onward_copy(place - 1).start()

        prepare(final, late)

    joins = [*range(1, owned), *[None] * (owned + 1)]
    for place in range(owned):
        run_position(place, *joins[2 * place : 2 * place + 2])

    for place in range(straight, owned):
        await_near(place)

    for index, ref in (
        (0, own_out),
        (1, intensity_out),
        (3, joined.at[:, others]),
        (4, own_back),
        (5, rim_back.at[:, others]),
    ):
        sent(index, ref)

    arrived(own_terms, last_sems.at[0])

    @pl.when(has_outward)
    def _():
        sent(2, relay_out)
        arrived(far_terms, last_sems.at[1])

    @pl.when(has_inward)
    def _():
        sent(6, far_terms)


def exchange(sections, peers, offsets, layer, probe, intensity):
    positions, extent = (intensity.shape[0], intensity.shape[-1])
    strip, columns = layer.shape[1:]
    blocks = columns // extent
    owned = positions // sections
    hbm = pl.BlockSpec(memory_space=pltpu.HBM)
    smem = pl.BlockSpec(memory_space=pltpu.SMEM)
    tables = jnp.asarray(block_tables(extent))
    by_place = (owned, sections, 2, strip, extent)
    by_owner = (sections, owned, 2, strip, extent)
    first = (sections, 2, strip, extent)
    buffers = (by_owner, by_owner, by_place, by_place, by_place, by_place, first, first)
    buffers += (by_place, by_place)
    per_place = pltpu.SemaphoreType.DMA((owned,))
    out = pl.pallas_call(
        functools.partial(exchange_kernel, sections, peers),
        out_shape=[jax.ShapeDtypeStruct(by_place, jnp.bfloat16)] * 3
        + [jax.ShapeDtypeStruct((2, positions), jnp.int32)] * 3,
        in_specs=[hbm] * 5,
        out_specs=[hbm] * 3 + [smem] * 3,
        scratch_shapes=[
            pltpu.VMEM((blocks, 2, strip, extent), jnp.float32),
            pltpu.VMEM(probe.shape, jnp.float32),
            pltpu.VMEM((owned, extent, extent), jnp.float32),
            pltpu.VMEM((owned, extent, extent), jnp.bfloat16),
            pltpu.VMEM((owned, extent, extent), jnp.bfloat16),
            pltpu.VMEM(tables.shape, jnp.bfloat16),
            *[pltpu.VMEM(shape, jnp.bfloat16) for shape in buffers],
            *[pltpu.VMEM((sections, 2, extent, extent), jnp.float32)] * 2,
            *[pltpu.VMEM((2, extent, extent), jnp.float32)] * 2,
            pltpu.SemaphoreType.DMA((5,)),
            pltpu.SemaphoreType.DMA((2,)),
            pltpu.SemaphoreType.DMA((2,)),
            pltpu.SemaphoreType.DMA((7,)),
            *[per_place] * 6,
            pltpu.SemaphoreType.DMA((2,)),
        ],
        compiler_params=pltpu.CompilerParams(
            collective_id=0, has_side_effects=True, vmem_limit_bytes=56 * 1024 * 1024
        ),
        name="exchange",
    )(offsets, layer, probe, intensity, tables)
    return out[:3], out[3:]


def scatter_kernel(
    peers,
    sections,
    own_places_hbm,
    near_places_hbm,
    far_places_hbm,
    own_hbm,
    near_hbm,
    far_hbm,
    out_hbm,
    own_places,
    near_places,
    far_places,
    own_ref,
    near_ref,
    far_ref,
    total_real,
    total_imag,
    load_sems,
    store_sems,
):
    scan = lax.axis_index("scan")
    positions = own_ref.shape[0]
    strip, extent = own_ref.shape[2:]
    totals = (total_real, total_imag)
    columns = total_real.shape[1]
    even = jnp.where(lax.rem(scan, 2) == 0, 1, 0)
    odd = 1 - even
    partner = scan + even - odd
    far = scan - even + odd
    has_far = (far >= 0) & (far < peers)

    loads = [
        pltpu.make_async_copy(source, target, load_sems.at[i])
        for i, (source, target) in enumerate(
            (
                (own_places_hbm, own_places),
                (near_places_hbm, near_places),
                (far_places_hbm, far_places),
                (own_hbm, own_ref),
                (near_hbm, near_ref),
                (far_hbm, far_ref),
            )
        )
    ]
    for load in loads:
        load.start()
    for total in totals:
        total[...] = jnp.zeros_like(total)
    lanes = lax.broadcasted_iota(jnp.int32, (strip, extent), 1)

    def add(source, index, column, keep):
        first, second, shift = column_blocks(column, extent, columns)
        ahead = lanes >= shift
        terms = [source[index, part].astype(jnp.float32) for part in range(2)]
        if keep is not None:
            terms = [jnp.where(keep, term, 0.0) for term in terms]
        for start, chosen in ((first, ahead), (second, jnp.logical_not(ahead))):
            place = (slice(None), pl.ds(start, extent))
            sums = [
                total[place] + jnp.where(chosen, term, 0.0) for total, term in zip(totals, terms)
            ]
            for total, value in zip(totals, sums):
                total[place] = value

    def add_all(source, places, neighbour, above):
        def step(index, carry):
            owner, place = (lax.rem(index, sections), lax.div(index, sections))
            position = owner * (positions // sections) + place
            row = places[0, position] - (neighbour - 1) * strip
            keep = None if above is None else kept_rows((strip, extent), row, above)
            add(source, index, places[1, position], keep)
            return carry

        lax.fori_loop(0, positions, step, 0, unroll=4)

    loads[0].wait()
    loads[3].wait()
    add_all(own_ref, own_places, scan, None)
    loads[1].wait()
    loads[4].wait()
    add_all(near_ref, near_places, partner, even)
    loads[2].wait()
    loads[5].wait()

    @pl.when(has_far)
    def _():
        add_all(far_ref, far_places, far, odd)

    stores = [
        pltpu.make_async_copy(total, out_hbm.at[part], store_sems.at[part])
        for part, total in enumerate(totals)
    ]
    for store in stores:
        store.start()
    for store in stores:
        store.wait()


def scatter(peers, sections, places, terms, strip, columns):
    hbm = pl.BlockSpec(memory_space=pltpu.HBM)
    terms = [term.reshape(-1, *term.shape[-3:]) for term in terms]
    return pl.pallas_call(
        functools.partial(scatter_kernel, peers, sections),
        out_shape=jax.ShapeDtypeStruct((2, strip, columns), jnp.float32),
        in_specs=[hbm] * 6,
        out_specs=hbm,
        scratch_shapes=[pltpu.SMEM(place.shape, place.dtype) for place in places]
        + [pltpu.VMEM(term.shape, term.dtype) for term in terms]
        + [
            pltpu.VMEM((strip, columns), jnp.float32),
            pltpu.VMEM((strip, columns), jnp.float32),
            pltpu.SemaphoreType.DMA((6,)),
            pltpu.SemaphoreType.DMA((2,)),
        ],
        compiler_params=pltpu.CompilerParams(vmem_limit_bytes=56 * 1024 * 1024),
        name="scatter",
    )(*places, *terms)


def shards(peers, sections, object_slices, probe_wave, offsets, intensity):
    layer = object_slices[0]
    strip, columns = layer.shape[1:]
    places = offsets.T
    terms, taken = exchange(sections, peers, places, layer, probe_wave, intensity)
    return scatter(peers, sections, taken, terms, strip, columns)[None]


def solution(mesh):
    in_specs = (P("depth", None, "scan", None), P(), P("scan", None), P("scan", None, None))
    out_specs = P("depth", None, "scan", None)
    body = functools.partial(shards, mesh.shape["scan"], mesh.shape["depth"])
    return jax.shard_map(body, mesh=mesh, in_specs=in_specs, out_specs=out_specs, check_vma=False)
```

```python
import functools
import math

import jax
import jax.numpy as jnp
import numpy as np
from jax import lax
from jax.experimental import pallas as pl
from jax.experimental.pallas import tpu as pltpu
from jax.sharding import PartitionSpec as P

FRESNEL = 0.0024
MESH = pl.DeviceIdType.MESH
HOP, HOP_CONJ, FOURIER, FOURIER_CONJ = range(4)
CONJUGATE_OF = {HOP: HOP_CONJ, HOP_CONJ: HOP, FOURIER: FOURIER_CONJ, FOURIER_CONJ: FOURIER}


def block_tables(extent):
    index = np.arange(extent)
    fourier = np.exp(-2j * math.pi / extent * (index[:, None] * index[None, :] % extent))
    fourier = fourier / math.sqrt(extent)
    signed = np.where(index < extent // 2, index, index - extent).astype(np.float64)
    phase = np.exp(-1j * math.pi * FRESNEL * signed * signed)
    hop = (fourier.conj() * phase[None, :]) @ fourier
    tables = []
    for matrix in (hop, hop.conj(), fourier, fourier.conj()):
        real, imag = (matrix.real, matrix.imag)
        block = np.block([[real, imag], [-imag, real]]).astype(np.float32)
        high = block.astype(jnp.bfloat16)
        tables.append(np.stack([high, (block - high.astype(np.float32)).astype(jnp.bfloat16)]))
    return np.stack(tables)


def times(first, second):
    return (
        first[0] * second[0] - first[1] * second[1],
        first[0] * second[1] + first[1] * second[0],
    )


def conj_times(first, second):
    return (
        first[0] * second[0] + first[1] * second[1],
        first[0] * second[1] - first[1] * second[0],
    )


def split(value):
    high = value.astype(jnp.bfloat16)
    return high, (value - high.astype(jnp.float32)).astype(jnp.bfloat16)


def dot(first, second):
    return jnp.dot(first, second, preferred_element_type=jnp.float32)


def right_product(fields, high, low, passes):
    extent = fields[0][0].shape[1]
    rows = [jnp.concatenate(field, axis=1) for field in fields]
    value = jnp.concatenate(rows, axis=0)
    if passes == 1:
        out = dot(value.astype(jnp.bfloat16), high)
    else:
        value_high, value_low = split(value)
        out = dot(value_high, high) + dot(value_low, high) + dot(value_high, low)
    picks = [slice(i * extent, (i + 1) * extent) for i in range(len(fields))]
    return [(out[pick, :extent], out[pick, extent:]) for pick in picks]


def left_product(fields, high, low, passes):
    extent = fields[0][0].shape[0]
    columns = [jnp.concatenate(field, axis=0) for field in fields]
    value = jnp.concatenate(columns, axis=1)
    value_high, value_low = split(value)
    if passes == 1:
        out = dot(high, value_high)
    elif len(fields) == 1:
        both = dot(high, jnp.concatenate([value_high, value_low], axis=1))
        out = both[:, :extent] + both[:, extent:] + dot(low, value_high)
    else:
        out = dot(high, value_high) + dot(high, value_low) + dot(low, value_high)
    picks = [slice(i * extent, (i + 1) * extent) for i in range(len(fields))]
    return [(out[:extent, pick], out[extent:, pick]) for pick in picks]


def transform(fields, tables_ref, kind, passes=3):
    other = CONJUGATE_OF[kind]
    fields = right_product(fields, tables_ref[kind, 0], tables_ref[kind, 1], passes)
    return left_product(fields, tables_ref[other, 0], tables_ref[other, 1], passes)


def split_column(column, extent):
    return lax.shift_right_logical(column, extent.bit_length() - 1), column & (extent - 1)


def column_blocks(column, extent, columns):
    block, shift = split_column(column, extent)
    following = jnp.minimum(block + 1, columns // extent - 1)
    first = pl.multiple_of(block * extent, extent)
    return first, pl.multiple_of(following * extent, extent), shift


def kept_rows(shape, row, above):
    inside = lax.broadcasted_iota(jnp.int32, shape, 0) >= row
    return inside.astype(jnp.int32) == above


def exchange_kernel(
    sections,
    peers,
    offsets_hbm,
    layer_hbm,
    probe_hbm,
    intensity_hbm,
    tables_hbm,
    own_terms,
    near_terms,
    far_terms,
    near_places_hbm,
    far_places_hbm,
    own_places,
    near_places,
    far_places,
    layer,
    probe,
    intensity,
    intensity_out,
    intensity_in,
    tables,
    own_out,
    own_in,
    relay_out,
    relay_in,
    joined,
    rim_in,
    near_first,
    far_first,
    own_back,
    rim_back,
    waves_even,
    waves_odd,
    adjoint_even,
    adjoint_odd,
    load_sems,
    store_sems,
    place_send,
    place_recv,
    send_sems,
    intensity_recv,
    own_recv,
    relay_recv,
    rim_recv,
    near_recv,
    kept_sems,
    last_sems,
):
    waves, adjoint = ((waves_even, waves_odd), (adjoint_even, adjoint_odd))
    section = lax.axis_index("depth")
    scan = lax.axis_index("scan")
    even = jnp.where(lax.rem(scan, 2) == 0, 1, 0)
    odd = 1 - even
    partner = scan + even - odd
    far = scan - even + odd
    outward = scan - 2 * even + 2 * odd
    inward = scan + 2 * even - 2 * odd
    has_outward = (outward >= 0) & (outward < peers)
    has_inward = (inward >= 0) & (inward < peers)
    blocks, _, strip, extent = layer.shape
    owned = intensity.shape[0]
    last = owned - 1
    straight = max(0, owned - 2)

    loads = [
        pltpu.make_async_copy(source, target, load_sems.at[i])
        for i, (source, target) in enumerate(
            (
                (probe_hbm, probe),
                (intensity_hbm.at[pl.ds(section * owned, owned)], intensity),
                (tables_hbm, tables),
                (offsets_hbm, own_places),
            )
        )
    ]

    def layer_load(block):
        columns = pl.ds(pl.multiple_of(block * extent, extent), extent)
        return pltpu.make_async_copy(
            layer_hbm.at[:, :, columns], layer.at[block], load_sems.at[4]
        )

    def start_layer(block, carry):
        layer_load(block).start()
        return carry

    loads[3].start()
    lax.fori_loop(0, blocks, start_layer, 0)
    for load in loads[:3]:
        load.start()

    barrier = pltpu.get_barrier_semaphore()

    def greet(**device):
        pl.semaphore_signal(barrier, inc=1, device_id=device, device_id_type=MESH)

    def greet_section(step, carry):
        other = lax.rem(section + step, sections)
        greet(scan=partner, depth=other)

        @pl.when(step > 0)
        def _():
            greet(depth=other)

        @pl.when(has_outward)
        def _():
            greet(scan=outward, depth=other)

        @pl.when(has_inward)
        def _():
            greet(scan=inward, depth=other)

        return carry

    lax.fori_loop(0, sections, greet_section, 0)

    @pl.when(has_outward)
    def _():
        greet(scan=far)

    @pl.when(jnp.logical_not(has_inward))
    def _():
        relay_in[...] = jnp.zeros_like(relay_in)
        far_first[...] = jnp.zeros_like(far_first)

    greeted = (
        2 * sections
        - 1
        + jnp.where(has_outward, sections + 1, 0)
        + jnp.where(has_inward, sections, 0)
    )
    loads[3].wait()
    pl.semaphore_wait(barrier, greeted)

    def remote(source, target, send, recv, device):
        return pltpu.make_async_remote_copy(
            src_ref=source,
            dst_ref=target,
            send_sem=send,
            recv_sem=recv,
            device_id=device,
            device_id_type=MESH,
        )

    near_place_copy = remote(
        own_places, near_places, place_send.at[0], place_recv.at[0], {"scan": partner}
    )
    far_place_copy = remote(
        own_places, far_places, place_send.at[1], place_recv.at[1], {"scan": far}
    )
    near_place_copy.start()

    @pl.when(has_outward)
    def _():
        far_place_copy.start()

    @pl.when(jnp.logical_not(has_outward))
    def _():
        def clear(index, carry):
            far_places[0, index] = 0
            far_places[1, index] = 0
            return carry

        lax.fori_loop(0, far_places.shape[1], clear, 0)

    def own_copy(owner, sender, first, count):
        return remote(
            own_out.at[owner, pl.ds(first, count)],
            own_in.at[sender, pl.ds(first, count)],
            send_sems.at[0],
            own_recv.at[first],
            {"scan": partner, "depth": owner},
        )

    def intensity_copy(first, count):
        return remote(
            intensity_out.at[pl.ds(first, count)],
            intensity_in.at[pl.ds(first, count)],
            send_sems.at[1],
            intensity_recv.at[first],
            {"scan": partner},
        )

    def relay_copy(place):
        return remote(
            relay_out.at[place],
            relay_in.at[place],
            send_sems.at[2],
            relay_recv.at[place],
            {"scan": outward},
        )

    def far_first_copy(owner):
        return remote(
            relay_out.at[0, owner],
            far_first.at[section],
            send_sems.at[2],
            relay_recv.at[0],
            {"scan": outward, "depth": owner},
        )

    def near_first_copy(owner):
        return remote(
            joined.at[0, owner],
            near_first.at[section],
            send_sems.at[3],
            rim_recv.at[0],
            {"depth": owner},
        )

    def rim_copy(owner, place):
        return remote(
            joined.at[place, owner],
            rim_in.at[place, section],
            send_sems.at[3],
            rim_recv.at[place],
            {"depth": owner},
        )

    def own_back_copy(target, place):
        return remote(
            own_back.at[place, target],
            own_terms.at[place, section],
            send_sems.at[4],
            last_sems.at[0],
            {"scan": partner, "depth": target},
        )

    def rim_back_copy(target, place):
        return remote(
            rim_back.at[place, target],
            near_terms.at[place, section],
            send_sems.at[5],
            near_recv.at[place],
            {"depth": target},
        )

    def keep_near(place):
        return pltpu.make_async_copy(
            rim_back.at[place, section], near_terms.at[place, section], kept_sems.at[place]
        )

    def onward_copy(place):
        return remote(
            near_terms.at[place],
            far_terms.at[place],
            send_sems.at[6],
            last_sems.at[1],
            {"scan": inward},
        )

    def far_last_copy(target, place):
        return remote(
            rim_back.at[place, target],
            far_terms.at[place, section],
            send_sems.at[6],
            last_sems.at[1],
            {"scan": inward, "depth": target},
        )

    def sent(index, ref):
        remote(ref, ref, send_sems.at[index], last_sems.at[0], {"scan": partner}).wait_send()

    def arrived(ref, sem):
        remote(ref, ref, send_sems.at[0], sem, {"scan": partner}).wait_recv()

    others = pl.ds(0, sections - 1)

    lanes = lax.broadcasted_iota(jnp.int32, (strip, extent), 1)

    def cut(column):
        first, shift = split_column(column, extent)
        second = jnp.minimum(first + 1, blocks - 1)
        ahead = lanes >= shift
        return [jnp.where(ahead, layer[first, part], layer[second, part]) for part in range(2)]

    order = [lax.rem(section + 1 + step, sections) for step in range(sections)]

    loads[1].wait()

    pltpu.make_async_copy(layer, layer, load_sems.at[4]).wait()

    def cut_own(place):
        for owner in order:
            for part, half in enumerate(cut(own_places[1, owner * owned + place])):
                own_out[owner, place, part] = half.astype(jnp.bfloat16)

    def send_own(first, count):
        lax.fori_loop(first, first + count, lambda place, carry: (cut_own(place), carry)[1], 0)
        for owner in order:
            own_copy(owner, section, first, count).start()

    def send_intensity(first, count):
        picked = pl.ds(first, count)
        intensity_out[picked] = intensity[picked].astype(jnp.bfloat16)
        intensity_copy(first, count).start()

    def cut_far(place):
        for owner in order:
            index = owner * owned + place
            keep = kept_rows((strip, extent), far_places[0, index] - (far - 1) * strip, odd)
            for part, half in enumerate(cut(far_places[1, index])):
                relay_out[place, owner, part] = jnp.where(keep, half, 0.0).astype(jnp.bfloat16)

    def send_relay(place, carry):
        cut_far(place)
        relay_copy(place).start()
        return carry

    def near_kept(index):
        row = near_places[0, index] - (partner - 1) * strip
        return kept_rows((strip, extent), row, even)

    def send_near_first():
        for owner in order:
            for part, half in enumerate(cut(near_places[1, owner * owned])):
                joined[0, owner, part] = half.astype(jnp.bfloat16)
        near_first[section] = joined[0, section]
        for owner in order[:-1]:
            near_first_copy(owner).start()

    def await_relay(place):
        @pl.when(has_inward)
        def _():
            arrived(relay_in.at[place], relay_recv.at[place])

    def send_rim(owner, place):
        index = owner * owned + place
        keep = near_kept(index)
        for part, half in enumerate(cut(near_places[1, index])):
            passed = relay_in[place, owner, part].astype(jnp.float32)
            joined[place, owner, part] = jnp.where(keep, half, passed).astype(jnp.bfloat16)

        @pl.when(owner != section)
        def _():
            rim_copy(owner, place).start()

        @pl.when(owner == section)
        def _():
            rim_in[place, section] = joined[place, section]

    chunks = [(first, 1) for first in range(min(owned, 2))]
    if owned > 2:
        chunks.append((2, owned - 2))
    for first, count in chunks:
        send_own(first, count)
        send_intensity(first, count)

    @pl.when(has_outward)
    def _():
        far_place_copy.wait()
        cut_far(0)
        for owner in order:
            far_first_copy(owner).start()

    near_place_copy.wait()
    place_stores = [
        pltpu.make_async_copy(source, target, store_sems.at[i])
        for i, (source, target) in enumerate(
            ((near_places, near_places_hbm), (far_places, far_places_hbm))
        )
    ]
    for place_store in place_stores:
        place_store.start()
    send_near_first()

    @pl.when(has_outward)
    def _():
        lax.fori_loop(1, owned, send_relay, 0)

    loads[0].wait()
    loads[2].wait()

    def join_first():
        arrived(near_first.at[others], rim_recv.at[0])

        @pl.when(has_inward)
        def _():
            arrived(far_first, relay_recv.at[0])

        keep = near_kept(section * owned)

        def join_slice(slice_index, carry):
            for part in range(2):
                here = near_first[slice_index, part].astype(jnp.float32)
                passed = far_first[slice_index, part].astype(jnp.float32)
                rim_in[0, slice_index, part] = jnp.where(keep, here, passed).astype(jnp.bfloat16)
            return carry

        lax.fori_loop(0, sections, join_slice, 0)

    def patch(slice_index, place):
        return tuple(
            jnp.concatenate(
                [own_in[slice_index, place, part], rim_in[place, slice_index, part]], axis=0
            ).astype(jnp.float32)
            for part in range(2)
        )

    def stored(ref, *place):
        return (ref[(*place, 0)], ref[(*place, 1)])

    def store(ref, place, field):
        for part in range(2):
            ref[(*place, part)] = field[part]

    final = sections - 1

    def await_near(place):
        arrived(near_terms.at[place, others], near_recv.at[place])
        keep_near(place).wait()

    def prepare(step, place):
        if place is not None:
            if isinstance(step, int):
                if step == 0:
                    await_relay(place)
            else:
                pl.when(step == 0)(lambda: await_relay(place))

            send_rim(lax.rem(section + 1 + step, sections), place)

    def begin(place):
        if place == 0:
            join_first()
        else:
            arrived(rim_in.at[place, others], rim_recv.at[place])
        index = section * owned + place
        down = near_places[0, index] - (partner - 2) * strip
        right = lax.rem(near_places[1, index], extent)
        rolled = [pltpu.roll(probe[part], lax.rem(down, extent), 0) for part in range(2)]
        store(waves[place % 2], (0,), [pltpu.roll(value, right, 1) for value in rolled])
        for first, count in chunks:
            if first == place:
                arrived(own_in.at[:, pl.ds(first, count)], own_recv.at[first])

    def excite(place, slice_index):
        return times(patch(slice_index, place), stored(waves[place % 2], slice_index))

    def forward(place, slice_index):
        return transform([excite(place, slice_index)], tables, HOP)[0]

    def turn(place):
        (real, imag), = transform([excite(place, final)], tables, FOURIER)
        for first, count in chunks:
            if first == place:
                intensity_copy(first, count).wait_recv()
        misfit = real * real + imag * imag - intensity_in[place].astype(jnp.float32)
        driven = (misfit * real, misfit * imag)
        store(adjoint[place % 2], (), transform([driven], tables, FOURIER_CONJ)[0])

    def give(place, slice_index):
        term = conj_times(stored(waves[place % 2], slice_index), stored(adjoint[place % 2]))
        for part in range(2):
            value = term[part].astype(jnp.bfloat16)
            own_back[place, slice_index, part] = value[:strip]
            rim_back[place, slice_index, part] = value[strip:]

        if place >= straight:

            @pl.when(has_inward)
            def _():
                far_last_copy(slice_index, place).start()

        @pl.when(slice_index != section)
        def _():
            rim_back_copy(slice_index, place).start()

        @pl.when(slice_index == section)
        def _():
            keep_near(place).start()

        own_back_copy(slice_index, place).start()

    def backward(place, slice_index):
        masked = conj_times(patch(slice_index, place), stored(adjoint[place % 2]))
        return transform([masked], tables, HOP_CONJ, passes=1)[0]

    def run_position(place, early, late):
        begin(place)

        def forward_step(index, carry):
            store(waves[place % 2], (index + 1,), forward(place, index))
            return carry

        lax.fori_loop(0, final, forward_step, 0)
        for index in range(sections):
            prepare(index, early)
        turn(place)

        def backward_step(index, carry):
            give(place, final - index)
            store(adjoint[place % 2], (), backward(place, final - index))
            prepare(index, late)
            return carry

        lax.fori_loop(0, final, backward_step, 0)
        give(place, 0)
        if 0 < place <= straight:
            await_near(place - 1)

            @pl.when(has_inward)
            def _():
                onward_copy(place - 1).start()

        prepare(final, late)

    joins = [*range(1, owned), *[None] * (owned + 1)]
    for place in range(owned):
        run_position(place, *joins[2 * place : 2 * place + 2])

    for place in range(straight, owned):
        await_near(place)

    for place_store in place_stores:
        place_store.wait()

    for index, ref in (
        (0, own_out),
        (1, intensity_out),
        (3, joined.at[:, others]),
        (4, own_back),
        (5, rim_back.at[:, others]),
    ):
        sent(index, ref)

    arrived(own_terms, last_sems.at[0])

    @pl.when(has_outward)
    def _():
        sent(2, relay_out)
        arrived(far_terms, last_sems.at[1])

    @pl.when(has_inward)
    def _():
        sent(6, far_terms)


def exchange(sections, peers, offsets, layer, probe, intensity):
    positions, extent = (intensity.shape[0], intensity.shape[-1])
    strip, columns = layer.shape[1:]
    blocks = columns // extent
    owned = positions // sections
    hbm = pl.BlockSpec(memory_space=pltpu.HBM)
    tables = jnp.asarray(block_tables(extent))
    by_place = (owned, sections, 2, strip, extent)
    by_owner = (sections, owned, 2, strip, extent)
    first = (sections, 2, strip, extent)
    buffers = (by_owner, by_owner, by_place, by_place, by_place, by_place, first, first)
    buffers += (by_place, by_place)
    per_place = pltpu.SemaphoreType.DMA((owned,))
    out = pl.pallas_call(
        functools.partial(exchange_kernel, sections, peers),
        out_shape=[jax.ShapeDtypeStruct(by_place, jnp.bfloat16)] * 3
        + [jax.ShapeDtypeStruct((2, positions), jnp.int32)] * 2,
        in_specs=[hbm] * 5,
        out_specs=[hbm] * 5,
        scratch_shapes=[
            *[pltpu.SMEM((2, positions), jnp.int32)] * 3,
            pltpu.VMEM((blocks, 2, strip, extent), jnp.float32),
            pltpu.VMEM(probe.shape, jnp.float32),
            pltpu.VMEM((owned, extent, extent), jnp.float32),
            pltpu.VMEM((owned, extent, extent), jnp.bfloat16),
            pltpu.VMEM((owned, extent, extent), jnp.bfloat16),
            pltpu.VMEM(tables.shape, jnp.bfloat16),
            *[pltpu.VMEM(shape, jnp.bfloat16) for shape in buffers],
            *[pltpu.VMEM((sections, 2, extent, extent), jnp.float32)] * 2,
            *[pltpu.VMEM((2, extent, extent), jnp.float32)] * 2,
            pltpu.SemaphoreType.DMA((5,)),
            pltpu.SemaphoreType.DMA((2,)),
            pltpu.SemaphoreType.DMA((2,)),
            pltpu.SemaphoreType.DMA((2,)),
            pltpu.SemaphoreType.DMA((7,)),
            *[per_place] * 6,
            pltpu.SemaphoreType.DMA((2,)),
        ],
        compiler_params=pltpu.CompilerParams(
            collective_id=0, has_side_effects=True, vmem_limit_bytes=56 * 1024 * 1024
        ),
        name="exchange",
    )(offsets, layer, probe, intensity, tables)
    return out[:3], [offsets, *out[3:]]


def scatter_kernel(
    peers,
    sections,
    own_places_hbm,
    near_places_hbm,
    far_places_hbm,
    own_hbm,
    near_hbm,
    far_hbm,
    out_hbm,
    own_places,
    near_places,
    far_places,
    own_ref,
    near_ref,
    far_ref,
    total_real,
    total_imag,
    load_sems,
    store_sems,
):
    scan = lax.axis_index("scan")
    positions = own_ref.shape[0]
    strip, extent = own_ref.shape[2:]
    totals = (total_real, total_imag)
    columns = total_real.shape[1]
    even = jnp.where(lax.rem(scan, 2) == 0, 1, 0)
    odd = 1 - even
    partner = scan + even - odd
    far = scan - even + odd
    has_far = (far >= 0) & (far < peers)

    loads = [
        pltpu.make_async_copy(source, target, load_sems.at[i])
        for i, (source, target) in enumerate(
            (
                (own_places_hbm, own_places),
                (near_places_hbm, near_places),
                (far_places_hbm, far_places),
                (own_hbm, own_ref),
                (near_hbm, near_ref),
                (far_hbm, far_ref),
            )
        )
    ]
    for load in loads:
        load.start()
    for total in totals:
        total[...] = jnp.zeros_like(total)
    lanes = lax.broadcasted_iota(jnp.int32, (strip, extent), 1)

    def add(source, index, column, keep):
        first, second, shift = column_blocks(column, extent, columns)
        ahead = lanes >= shift
        terms = [source[index, part].astype(jnp.float32) for part in range(2)]
        if keep is not None:
            terms = [jnp.where(keep, term, 0.0) for term in terms]
        for start, chosen in ((first, ahead), (second, jnp.logical_not(ahead))):
            place = (slice(None), pl.ds(start, extent))
            sums = [
                total[place] + jnp.where(chosen, term, 0.0) for total, term in zip(totals, terms)
            ]
            for total, value in zip(totals, sums):
                total[place] = value

    def add_all(source, places, neighbour, above):
        def step(index, carry):
            owner, place = (lax.rem(index, sections), lax.div(index, sections))
            position = owner * (positions // sections) + place
            row = places[0, position] - (neighbour - 1) * strip
            keep = None if above is None else kept_rows((strip, extent), row, above)
            add(source, index, places[1, position], keep)
            return carry

        lax.fori_loop(0, positions, step, 0, unroll=4)

    loads[0].wait()
    loads[3].wait()
    add_all(own_ref, own_places, scan, None)
    loads[1].wait()
    loads[4].wait()
    add_all(near_ref, near_places, partner, even)
    loads[2].wait()
    loads[5].wait()

    @pl.when(has_far)
    def _():
        add_all(far_ref, far_places, far, odd)

    stores = [
        pltpu.make_async_copy(total, out_hbm.at[part], store_sems.at[part])
        for part, total in enumerate(totals)
    ]
    for store in stores:
        store.start()
    for store in stores:
        store.wait()


def scatter(peers, sections, places, terms, strip, columns):
    hbm = pl.BlockSpec(memory_space=pltpu.HBM)
    terms = [term.reshape(-1, *term.shape[-3:]) for term in terms]
    return pl.pallas_call(
        functools.partial(scatter_kernel, peers, sections),
        out_shape=jax.ShapeDtypeStruct((2, strip, columns), jnp.float32),
        in_specs=[hbm] * 6,
        out_specs=hbm,
        scratch_shapes=[pltpu.SMEM(place.shape, place.dtype) for place in places]
        + [pltpu.VMEM(term.shape, term.dtype) for term in terms]
        + [
            pltpu.VMEM((strip, columns), jnp.float32),
            pltpu.VMEM((strip, columns), jnp.float32),
            pltpu.SemaphoreType.DMA((6,)),
            pltpu.SemaphoreType.DMA((2,)),
        ],
        compiler_params=pltpu.CompilerParams(vmem_limit_bytes=56 * 1024 * 1024),
        name="scatter",
    )(*places, *terms)


def shards(peers, sections, object_slices, probe_wave, offsets, intensity):
    layer = object_slices[0]
    strip, columns = layer.shape[1:]
    places = offsets.T
    terms, taken = exchange(sections, peers, places, layer, probe_wave, intensity)
    return scatter(peers, sections, taken, terms, strip, columns)[None]


def solution(mesh):
    in_specs = (P("depth", None, "scan", None), P(), P("scan", None), P("scan", None, None))
    out_specs = P("depth", None, "scan", None)
    body = functools.partial(shards, mesh.shape["scan"], mesh.shape["depth"])
    return jax.shard_map(body, mesh=mesh, in_specs=in_specs, out_specs=out_specs, check_vma=False)
```

```python
import functools
import math

import jax
import jax.numpy as jnp
import numpy as np
from jax import lax
from jax.experimental import pallas as pl
from jax.experimental.pallas import tpu as pltpu
from jax.sharding import PartitionSpec as P

FRESNEL = 0.0024
MESH = pl.DeviceIdType.MESH
HOP, HOP_CONJ, FOURIER, FOURIER_CONJ = range(4)
CONJUGATE_OF = {HOP: HOP_CONJ, HOP_CONJ: HOP, FOURIER: FOURIER_CONJ, FOURIER_CONJ: FOURIER}


def block_tables(extent):
    index = np.arange(extent)
    fourier = np.exp(-2j * math.pi / extent * (index[:, None] * index[None, :] % extent))
    fourier = fourier / math.sqrt(extent)
    signed = np.where(index < extent // 2, index, index - extent).astype(np.float64)
    phase = np.exp(-1j * math.pi * FRESNEL * signed * signed)
    hop = (fourier.conj() * phase[None, :]) @ fourier
    tables = []
    for matrix in (hop, hop.conj(), fourier, fourier.conj()):
        real, imag = (matrix.real, matrix.imag)
        block = np.block([[real, imag], [-imag, real]]).astype(np.float32)
        high = block.astype(jnp.bfloat16)
        tables.append(np.stack([high, (block - high.astype(np.float32)).astype(jnp.bfloat16)]))
    return np.stack(tables)


def times(first, second):
    return (
        first[0] * second[0] - first[1] * second[1],
        first[0] * second[1] + first[1] * second[0],
    )


def conj_times(first, second):
    return (
        first[0] * second[0] + first[1] * second[1],
        first[0] * second[1] - first[1] * second[0],
    )


def split(value):
    high = value.astype(jnp.bfloat16)
    return high, (value - high.astype(jnp.float32)).astype(jnp.bfloat16)


def dot(first, second):
    return jnp.dot(first, second, preferred_element_type=jnp.float32)


def right_product(fields, high, low, passes):
    extent = fields[0][0].shape[1]
    rows = [jnp.concatenate(field, axis=1) for field in fields]
    value = jnp.concatenate(rows, axis=0)
    if passes == 1:
        out = dot(value.astype(jnp.bfloat16), high)
    else:
        value_high, value_low = split(value)
        out = dot(value_high, high) + dot(value_low, high) + dot(value_high, low)
    picks = [slice(i * extent, (i + 1) * extent) for i in range(len(fields))]
    return [(out[pick, :extent], out[pick, extent:]) for pick in picks]


def left_product(fields, high, low, passes):
    extent = fields[0][0].shape[0]
    columns = [jnp.concatenate(field, axis=0) for field in fields]
    value = jnp.concatenate(columns, axis=1)
    value_high, value_low = split(value)
    if passes == 1:
        out = dot(high, value_high)
    elif len(fields) == 1:
        both = dot(high, jnp.concatenate([value_high, value_low], axis=1))
        out = both[:, :extent] + both[:, extent:] + dot(low, value_high)
    else:
        out = dot(high, value_high) + dot(high, value_low) + dot(low, value_high)
    picks = [slice(i * extent, (i + 1) * extent) for i in range(len(fields))]
    return [(out[:extent, pick], out[extent:, pick]) for pick in picks]


def transform(fields, tables_ref, kind, passes=3):
    other = CONJUGATE_OF[kind]
    fields = right_product(fields, tables_ref[kind, 0], tables_ref[kind, 1], passes)
    return left_product(fields, tables_ref[other, 0], tables_ref[other, 1], passes)


def split_column(column, extent):
    return lax.shift_right_logical(column, extent.bit_length() - 1), column & (extent - 1)


def column_blocks(column, extent, columns):
    block, shift = split_column(column, extent)
    following = jnp.minimum(block + 1, columns // extent - 1)
    first = pl.multiple_of(block * extent, extent)
    return first, pl.multiple_of(following * extent, extent), shift


def kept_rows(shape, row, above):
    inside = lax.broadcasted_iota(jnp.int32, shape, 0) >= row
    return inside.astype(jnp.int32) == above


def exchange_kernel(
    sections,
    peers,
    offsets_hbm,
    layer_hbm,
    probe_hbm,
    intensity_hbm,
    tables_hbm,
    own_terms,
    near_terms,
    far_terms,
    near_places_hbm,
    far_places_hbm,
    own_places,
    near_places,
    far_places,
    layer,
    probe,
    intensity,
    intensity_out,
    intensity_in,
    tables,
    own_out,
    own_in,
    relay_out,
    relay_in,
    joined,
    rim_in,
    near_first,
    far_first,
    own_back,
    rim_back,
    waves_even,
    waves_odd,
    adjoint_even,
    adjoint_odd,
    load_sems,
    store_sems,
    place_send,
    place_recv,
    send_sems,
    intensity_recv,
    own_recv,
    relay_recv,
    rim_recv,
    near_recv,
    kept_sems,
    last_sems,
):
    waves, adjoint = ((waves_even, waves_odd), (adjoint_even, adjoint_odd))
    section = lax.axis_index("depth")
    scan = lax.axis_index("scan")
    even = jnp.where(lax.rem(scan, 2) == 0, 1, 0)
    odd = 1 - even
    partner = scan + even - odd
    far = scan - even + odd
    outward = scan - 2 * even + 2 * odd
    inward = scan + 2 * even - 2 * odd
    has_outward = (outward >= 0) & (outward < peers)
    has_inward = (inward >= 0) & (inward < peers)
    blocks, _, strip, extent = layer.shape
    owned = intensity.shape[0]
    last = owned - 1
    straight = max(0, owned - 2)

    loads = [
        pltpu.make_async_copy(source, target, load_sems.at[i])
        for i, (source, target) in enumerate(
            (
                (probe_hbm, probe),
                (intensity_hbm.at[pl.ds(section * owned, owned)], intensity),
                (tables_hbm, tables),
                (offsets_hbm, own_places),
            )
        )
    ]

    def layer_load(block):
        columns = pl.ds(pl.multiple_of(block * extent, extent), extent)
        return pltpu.make_async_copy(
            layer_hbm.at[:, :, columns], layer.at[block], load_sems.at[4]
        )

    def start_layer(block, carry):
        layer_load(block).start()
        return carry

    loads[3].start()
    lax.fori_loop(0, blocks, start_layer, 0)
    for load in loads[:3]:
        load.start()

    barrier = pltpu.get_barrier_semaphore()

    def greet(**device):
        pl.semaphore_signal(barrier, inc=1, device_id=device, device_id_type=MESH)

    def greet_section(step, carry):
        other = lax.rem(section + step, sections)
        greet(scan=partner, depth=other)

        @pl.when(step > 0)
        def _():
            greet(depth=other)

        @pl.when(has_outward)
        def _():
            greet(scan=outward, depth=other)

        @pl.when(has_inward)
        def _():
            greet(scan=inward, depth=other)

        return carry

    lax.fori_loop(0, sections, greet_section, 0)

    @pl.when(has_outward)
    def _():
        greet(scan=far)

    @pl.when(jnp.logical_not(has_inward))
    def _():
        relay_in[...] = jnp.zeros_like(relay_in)
        far_first[...] = jnp.zeros_like(far_first)

    greeted = (
        2 * sections
        - 1
        + jnp.where(has_outward, sections + 1, 0)
        + jnp.where(has_inward, sections, 0)
    )
    loads[3].wait()
    pl.semaphore_wait(barrier, greeted)

    def remote(source, target, send, recv, device):
        return pltpu.make_async_remote_copy(
            src_ref=source,
            dst_ref=target,
            send_sem=send,
            recv_sem=recv,
            device_id=device,
            device_id_type=MESH,
        )

    near_place_copy = remote(
        own_places, near_places, place_send.at[0], place_recv.at[0], {"scan": partner}
    )
    far_place_copy = remote(
        own_places, far_places, place_send.at[1], place_recv.at[1], {"scan": far}
    )
    near_place_copy.start()

    @pl.when(has_outward)
    def _():
        far_place_copy.start()

    @pl.when(jnp.logical_not(has_outward))
    def _():
        def clear(index, carry):
            far_places[0, index] = 0
            far_places[1, index] = 0
            return carry

        lax.fori_loop(0, far_places.shape[1], clear, 0)

    def own_copy(owner, sender, first, count):
        return remote(
            own_out.at[owner, pl.ds(first, count)],
            own_in.at[sender, pl.ds(first, count)],
            send_sems.at[0],
            own_recv.at[first],
            {"scan": partner, "depth": owner},
        )

    def intensity_copy(first, count):
        return remote(
            intensity_out.at[pl.ds(first, count)],
            intensity_in.at[pl.ds(first, count)],
            send_sems.at[1],
            intensity_recv.at[first],
            {"scan": partner},
        )

    def relay_copy(place):
        return remote(
            relay_out.at[place],
            relay_in.at[place],
            send_sems.at[2],
            relay_recv.at[place],
            {"scan": outward},
        )

    def far_first_copy(owner):
        return remote(
            relay_out.at[0, owner],
            far_first.at[section],
            send_sems.at[2],
            relay_recv.at[0],
            {"scan": outward, "depth": owner},
        )

    def near_first_copy(owner):
        return remote(
            joined.at[0, owner],
            near_first.at[section],
            send_sems.at[3],
            rim_recv.at[0],
            {"depth": owner},
        )

    def rim_copy(owner, place):
        return remote(
            joined.at[place, owner],
            rim_in.at[place, section],
            send_sems.at[3],
            rim_recv.at[place],
            {"depth": owner},
        )

    def own_back_copy(target, place):
        return remote(
            own_back.at[place, target],
            own_terms.at[place, section],
            send_sems.at[4],
            last_sems.at[0],
            {"scan": partner, "depth": target},
        )

    def rim_back_copy(target, place):
        return remote(
            rim_back.at[place, target],
            near_terms.at[place, section],
            send_sems.at[5],
            near_recv.at[place],
            {"depth": target},
        )

    def keep_near(place):
        return pltpu.make_async_copy(
            rim_back.at[place, section], near_terms.at[place, section], kept_sems.at[place]
        )

    def onward_copy(place):
        return remote(
            near_terms.at[place],
            far_terms.at[place],
            send_sems.at[6],
            last_sems.at[1],
            {"scan": inward},
        )

    def far_last_copy(target, place):
        return remote(
            rim_back.at[place, target],
            far_terms.at[place, section],
            send_sems.at[6],
            last_sems.at[1],
            {"scan": inward, "depth": target},
        )

    def sent(index, ref):
        remote(ref, ref, send_sems.at[index], last_sems.at[0], {"scan": partner}).wait_send()

    def arrived(ref, sem):
        remote(ref, ref, send_sems.at[0], sem, {"scan": partner}).wait_recv()

    others = pl.ds(0, sections - 1)

    lanes = lax.broadcasted_iota(jnp.int32, (strip, extent), 1)

    def cut(column):
        first, shift = split_column(column, extent)
        second = jnp.minimum(first + 1, blocks - 1)
        ahead = lanes >= shift
        return [jnp.where(ahead, layer[first, part], layer[second, part]) for part in range(2)]

    order = [lax.rem(section + 1 + step, sections) for step in range(sections)]

    loads[1].wait()

    pltpu.make_async_copy(layer, layer, load_sems.at[4]).wait()

    def cut_own(place):
        for owner in order:
            for part, half in enumerate(cut(own_places[1, owner * owned + place])):
                own_out[owner, place, part] = half.astype(jnp.bfloat16)

    def send_own(first, count):
        lax.fori_loop(first, first + count, lambda place, carry: (cut_own(place), carry)[1], 0)
        for owner in order:
            own_copy(owner, section, first, count).start()

    def send_intensity(first, count):
        picked = pl.ds(first, count)
        intensity_out[picked] = intensity[picked].astype(jnp.bfloat16)
        intensity_copy(first, count).start()

    def cut_far(place):
        for owner in order:
            index = owner * owned + place
            keep = kept_rows((strip, extent), far_places[0, index] - (far - 1) * strip, odd)
            for part, half in enumerate(cut(far_places[1, index])):
                relay_out[place, owner, part] = jnp.where(keep, half, 0.0).astype(jnp.bfloat16)

    def send_relay(place, carry):
        cut_far(place)
        relay_copy(place).start()
        return carry

    def near_kept(index):
        row = near_places[0, index] - (partner - 1) * strip
        return kept_rows((strip, extent), row, even)

    def send_near_first():
        for owner in order:
            for part, half in enumerate(cut(near_places[1, owner * owned])):
                joined[0, owner, part] = half.astype(jnp.bfloat16)
        near_first[section] = joined[0, section]
        for owner in order[:-1]:
            near_first_copy(owner).start()

    def await_relay(place):
        @pl.when(has_inward)
        def _():
            arrived(relay_in.at[place], relay_recv.at[place])

    def send_rim(owner, place):
        index = owner * owned + place
        keep = near_kept(index)
        for part, half in enumerate(cut(near_places[1, index])):
            passed = relay_in[place, owner, part].astype(jnp.float32)
            joined[place, owner, part] = jnp.where(keep, half, passed).astype(jnp.bfloat16)

        @pl.when(owner != section)
        def _():
            rim_copy(owner, place).start()

        @pl.when(owner == section)
        def _():
            rim_in[place, section] = joined[place, section]

    chunks = [(first, 1) for first in range(min(owned, 2))]
    if owned > 2:
        chunks.append((2, owned - 2))
    for first, count in chunks:
        send_own(first, count)
        send_intensity(first, count)

    @pl.when(has_outward)
    def _():
        far_place_copy.wait()
        cut_far(0)
        for owner in order:
            far_first_copy(owner).start()

    near_place_copy.wait()
    place_stores = [
        pltpu.make_async_copy(source, target, store_sems.at[i])
        for i, (source, target) in enumerate(
            ((near_places, near_places_hbm), (far_places, far_places_hbm))
        )
    ]
    for place_store in place_stores:
        place_store.start()
    send_near_first()

    @pl.when(has_outward)
    def _():
        lax.fori_loop(1, owned, send_relay, 0)

    loads[0].wait()
    loads[2].wait()

    def join_first():
        arrived(near_first.at[others], rim_recv.at[0])

        @pl.when(has_inward)
        def _():
            arrived(far_first, relay_recv.at[0])

        keep = near_kept(section * owned)

        def join_slice(slice_index, carry):
            for part in range(2):
                here = near_first[slice_index, part].astype(jnp.float32)
                passed = far_first[slice_index, part].astype(jnp.float32)
                rim_in[0, slice_index, part] = jnp.where(keep, here, passed).astype(jnp.bfloat16)
            return carry

        lax.fori_loop(0, sections, join_slice, 0)

    def patch(slice_index, place):
        return tuple(
            jnp.concatenate(
                [own_in[slice_index, place, part], rim_in[place, slice_index, part]], axis=0
            ).astype(jnp.float32)
            for part in range(2)
        )

    def stored(ref, *place):
        return (ref[(*place, 0)], ref[(*place, 1)])

    def store(ref, place, field):
        for part in range(2):
            ref[(*place, part)] = field[part]

    final = sections - 1

    def await_near(place):
        arrived(near_terms.at[place, others], near_recv.at[place])
        keep_near(place).wait()

    def prepare(step, place):
        if place is not None:
            if isinstance(step, int):
                if step == 0:
                    await_relay(place)
            else:
                pl.when(step == 0)(lambda: await_relay(place))

            send_rim(lax.rem(section + 1 + step, sections), place)

    def begin(place):
        if place == 0:
            join_first()
        else:
            arrived(rim_in.at[place, others], rim_recv.at[place])
        index = section * owned + place
        down = near_places[0, index] - (partner - 2) * strip
        right = lax.rem(near_places[1, index], extent)
        rolled = [pltpu.roll(probe[part], lax.rem(down, extent), 0) for part in range(2)]
        store(waves[place % 2], (0,), [pltpu.roll(value, right, 1) for value in rolled])
        for first, count in chunks:
            if first == place:
                arrived(own_in.at[:, pl.ds(first, count)], own_recv.at[first])

    def excite(place, slice_index):
        return times(patch(slice_index, place), stored(waves[place % 2], slice_index))

    def forward(place, slice_index):
        return transform([excite(place, slice_index)], tables, HOP)[0]

    def turn(place):
        (real, imag), = transform([excite(place, final)], tables, FOURIER)
        for first, count in chunks:
            if first == place:
                intensity_copy(first, count).wait_recv()
        misfit = real * real + imag * imag - intensity_in[place].astype(jnp.float32)
        driven = (misfit * real, misfit * imag)
        store(adjoint[place % 2], (), transform([driven], tables, FOURIER_CONJ)[0])

    def give(place, slice_index):
        term = conj_times(stored(waves[place % 2], slice_index), stored(adjoint[place % 2]))
        for part in range(2):
            value = term[part].astype(jnp.bfloat16)
            own_back[place, slice_index, part] = value[:strip]
            rim_back[place, slice_index, part] = value[strip:]

        if place >= straight:

            @pl.when(has_inward)
            def _():
                far_last_copy(slice_index, place).start()

        @pl.when(slice_index != section)
        def _():
            rim_back_copy(slice_index, place).start()

        @pl.when(slice_index == section)
        def _():
            keep_near(place).start()

        own_back_copy(slice_index, place).start()

    def backward(place, slice_index):
        masked = conj_times(patch(slice_index, place), stored(adjoint[place % 2]))
        return transform([masked], tables, HOP_CONJ, passes=1)[0]

    def run_position(place, early, late):
        begin(place)

        def forward_step(index, carry):
            store(waves[place % 2], (index + 1,), forward(place, index))
            return carry

        lax.fori_loop(0, final, forward_step, 0, unroll=True)
        for index in range(sections):
            prepare(index, early)
        turn(place)

        def backward_step(index, carry):
            give(place, final - index)
            store(adjoint[place % 2], (), backward(place, final - index))
            prepare(index, late)
            return carry

        lax.fori_loop(0, final, backward_step, 0)
        give(place, 0)
        if 0 < place <= straight:
            await_near(place - 1)

            @pl.when(has_inward)
            def _():
                onward_copy(place - 1).start()

        prepare(final, late)

    joins = [*range(1, owned), *[None] * (owned + 1)]
    for place in range(owned):
        run_position(place, *joins[2 * place : 2 * place + 2])

    for place in range(straight, owned):
        await_near(place)

    for place_store in place_stores:
        place_store.wait()

    for index, ref in (
        (0, own_out),
        (1, intensity_out),
        (3, joined.at[:, others]),
        (4, own_back),
        (5, rim_back.at[:, others]),
    ):
        sent(index, ref)

    arrived(own_terms, last_sems.at[0])

    @pl.when(has_outward)
    def _():
        sent(2, relay_out)
        arrived(far_terms, last_sems.at[1])

    @pl.when(has_inward)
    def _():
        sent(6, far_terms)


def exchange(sections, peers, offsets, layer, probe, intensity):
    positions, extent = (intensity.shape[0], intensity.shape[-1])
    strip, columns = layer.shape[1:]
    blocks = columns // extent
    owned = positions // sections
    hbm = pl.BlockSpec(memory_space=pltpu.HBM)
    tables = jnp.asarray(block_tables(extent))
    by_place = (owned, sections, 2, strip, extent)
    by_owner = (sections, owned, 2, strip, extent)
    first = (sections, 2, strip, extent)
    buffers = (by_owner, by_owner, by_place, by_place, by_place, by_place, first, first)
    buffers += (by_place, by_place)
    per_place = pltpu.SemaphoreType.DMA((owned,))
    out = pl.pallas_call(
        functools.partial(exchange_kernel, sections, peers),
        out_shape=[jax.ShapeDtypeStruct(by_place, jnp.bfloat16)] * 3
        + [jax.ShapeDtypeStruct((2, positions), jnp.int32)] * 2,
        in_specs=[hbm] * 5,
        out_specs=[hbm] * 5,
        scratch_shapes=[
            *[pltpu.SMEM((2, positions), jnp.int32)] * 3,
            pltpu.VMEM((blocks, 2, strip, extent), jnp.float32),
            pltpu.VMEM(probe.shape, jnp.float32),
            pltpu.VMEM((owned, extent, extent), jnp.float32),
            pltpu.VMEM((owned, extent, extent), jnp.bfloat16),
            pltpu.VMEM((owned, extent, extent), jnp.bfloat16),
            pltpu.VMEM(tables.shape, jnp.bfloat16),
            *[pltpu.VMEM(shape, jnp.bfloat16) for shape in buffers],
            *[pltpu.VMEM((sections, 2, extent, extent), jnp.float32)] * 2,
            *[pltpu.VMEM((2, extent, extent), jnp.float32)] * 2,
            pltpu.SemaphoreType.DMA((5,)),
            pltpu.SemaphoreType.DMA((2,)),
            pltpu.SemaphoreType.DMA((2,)),
            pltpu.SemaphoreType.DMA((2,)),
            pltpu.SemaphoreType.DMA((7,)),
            *[per_place] * 6,
            pltpu.SemaphoreType.DMA((2,)),
        ],
        compiler_params=pltpu.CompilerParams(
            collective_id=0, has_side_effects=True, vmem_limit_bytes=56 * 1024 * 1024
        ),
        name="exchange",
    )(offsets, layer, probe, intensity, tables)
    return out[:3], [offsets, *out[3:]]


def scatter_kernel(
    peers,
    sections,
    own_places_hbm,
    near_places_hbm,
    far_places_hbm,
    own_hbm,
    near_hbm,
    far_hbm,
    out_hbm,
    own_places,
    near_places,
    far_places,
    own_ref,
    near_ref,
    far_ref,
    total_real,
    total_imag,
    load_sems,
    store_sems,
):
    scan = lax.axis_index("scan")
    positions = own_ref.shape[0]
    strip, extent = own_ref.shape[2:]
    totals = (total_real, total_imag)
    columns = total_real.shape[1]
    even = jnp.where(lax.rem(scan, 2) == 0, 1, 0)
    odd = 1 - even
    partner = scan + even - odd
    far = scan - even + odd
    has_far = (far >= 0) & (far < peers)

    loads = [
        pltpu.make_async_copy(source, target, load_sems.at[i])
        for i, (source, target) in enumerate(
            (
                (own_places_hbm, own_places),
                (near_places_hbm, near_places),
                (far_places_hbm, far_places),
                (own_hbm, own_ref),
                (near_hbm, near_ref),
                (far_hbm, far_ref),
            )
        )
    ]
    for load in loads:
        load.start()
    for total in totals:
        total[...] = jnp.zeros_like(total)
    lanes = lax.broadcasted_iota(jnp.int32, (strip, extent), 1)

    def add(source, index, column, keep):
        first, second, shift = column_blocks(column, extent, columns)
        ahead = lanes >= shift
        terms = [source[index, part].astype(jnp.float32) for part in range(2)]
        if keep is not None:
            terms = [jnp.where(keep, term, 0.0) for term in terms]
        for start, chosen in ((first, ahead), (second, jnp.logical_not(ahead))):
            place = (slice(None), pl.ds(start, extent))
            sums = [
                total[place] + jnp.where(chosen, term, 0.0) for total, term in zip(totals, terms)
            ]
            for total, value in zip(totals, sums):
                total[place] = value

    def add_all(source, places, neighbour, above):
        def step(index, carry):
            owner, place = (lax.rem(index, sections), lax.div(index, sections))
            position = owner * (positions // sections) + place
            row = places[0, position] - (neighbour - 1) * strip
            keep = None if above is None else kept_rows((strip, extent), row, above)
            add(source, index, places[1, position], keep)
            return carry

        lax.fori_loop(0, positions, step, 0, unroll=4)

    loads[0].wait()
    loads[3].wait()
    add_all(own_ref, own_places, scan, None)
    loads[1].wait()
    loads[4].wait()
    add_all(near_ref, near_places, partner, even)
    loads[2].wait()
    loads[5].wait()

    @pl.when(has_far)
    def _():
        add_all(far_ref, far_places, far, odd)

    stores = [
        pltpu.make_async_copy(total, out_hbm.at[part], store_sems.at[part])
        for part, total in enumerate(totals)
    ]
    for store in stores:
        store.start()
    for store in stores:
        store.wait()


def scatter(peers, sections, places, terms, strip, columns):
    hbm = pl.BlockSpec(memory_space=pltpu.HBM)
    terms = [term.reshape(-1, *term.shape[-3:]) for term in terms]
    return pl.pallas_call(
        functools.partial(scatter_kernel, peers, sections),
        out_shape=jax.ShapeDtypeStruct((2, strip, columns), jnp.float32),
        in_specs=[hbm] * 6,
        out_specs=hbm,
        scratch_shapes=[pltpu.SMEM(place.shape, place.dtype) for place in places]
        + [pltpu.VMEM(term.shape, term.dtype) for term in terms]
        + [
            pltpu.VMEM((strip, columns), jnp.float32),
            pltpu.VMEM((strip, columns), jnp.float32),
            pltpu.SemaphoreType.DMA((6,)),
            pltpu.SemaphoreType.DMA((2,)),
        ],
        compiler_params=pltpu.CompilerParams(vmem_limit_bytes=56 * 1024 * 1024),
        name="scatter",
    )(*places, *terms)


def shards(peers, sections, object_slices, probe_wave, offsets, intensity):
    layer = object_slices[0]
    strip, columns = layer.shape[1:]
    places = offsets.T
    terms, taken = exchange(sections, peers, places, layer, probe_wave, intensity)
    return scatter(peers, sections, taken, terms, strip, columns)[None]


def solution(mesh):
    in_specs = (P("depth", None, "scan", None), P(), P("scan", None), P("scan", None, None))
    out_specs = P("depth", None, "scan", None)
    body = functools.partial(shards, mesh.shape["scan"], mesh.shape["depth"])
    return jax.shard_map(body, mesh=mesh, in_specs=in_specs, out_specs=out_specs, check_vma=False)
```

```python
import functools
import math

import jax
import jax.numpy as jnp
import numpy as np
from jax import lax
from jax.experimental import pallas as pl
from jax.experimental.pallas import tpu as pltpu
from jax.sharding import PartitionSpec as P

FRESNEL = 0.0024
MESH = pl.DeviceIdType.MESH
HOP, HOP_CONJ, FOURIER, FOURIER_CONJ = range(4)
CONJUGATE_OF = {HOP: HOP_CONJ, HOP_CONJ: HOP, FOURIER: FOURIER_CONJ, FOURIER_CONJ: FOURIER}


def block_tables(extent):
    index = np.arange(extent)
    fourier = np.exp(-2j * math.pi / extent * (index[:, None] * index[None, :] % extent))
    fourier = fourier / math.sqrt(extent)
    signed = np.where(index < extent // 2, index, index - extent).astype(np.float64)
    phase = np.exp(-1j * math.pi * FRESNEL * signed * signed)
    hop = (fourier.conj() * phase[None, :]) @ fourier
    tables = []
    for matrix in (hop, hop.conj(), fourier, fourier.conj()):
        real, imag = (matrix.real, matrix.imag)
        block = np.block([[real, imag], [-imag, real]]).astype(np.float32)
        high = block.astype(jnp.bfloat16)
        tables.append(np.stack([high, (block - high.astype(np.float32)).astype(jnp.bfloat16)]))
    return np.stack(tables)


def times(first, second):
    return (
        first[0] * second[0] - first[1] * second[1],
        first[0] * second[1] + first[1] * second[0],
    )


def conj_times(first, second):
    return (
        first[0] * second[0] + first[1] * second[1],
        first[0] * second[1] - first[1] * second[0],
    )


def split(value):
    high = value.astype(jnp.bfloat16)
    return high, (value - high.astype(jnp.float32)).astype(jnp.bfloat16)


def dot(first, second):
    return jnp.dot(first, second, preferred_element_type=jnp.float32)


def right_product(fields, high, low, passes):
    extent = fields[0][0].shape[1]
    rows = [jnp.concatenate(field, axis=1) for field in fields]
    value = jnp.concatenate(rows, axis=0)
    if passes == 1:
        out = dot(value.astype(jnp.bfloat16), high)
    else:
        value_high, value_low = split(value)
        out = dot(value_high, high) + dot(value_low, high) + dot(value_high, low)
    picks = [slice(i * extent, (i + 1) * extent) for i in range(len(fields))]
    return [(out[pick, :extent], out[pick, extent:]) for pick in picks]


def left_product(fields, high, low, passes):
    extent = fields[0][0].shape[0]
    columns = [jnp.concatenate(field, axis=0) for field in fields]
    value = jnp.concatenate(columns, axis=1)
    value_high, value_low = split(value)
    if passes == 1:
        out = dot(high, value_high)
    elif len(fields) == 1:
        both = dot(high, jnp.concatenate([value_high, value_low], axis=1))
        out = both[:, :extent] + both[:, extent:] + dot(low, value_high)
    else:
        out = dot(high, value_high) + dot(high, value_low) + dot(low, value_high)
    picks = [slice(i * extent, (i + 1) * extent) for i in range(len(fields))]
    return [(out[:extent, pick], out[extent:, pick]) for pick in picks]


def transform(fields, tables_ref, kind, passes=3):
    other = CONJUGATE_OF[kind]
    fields = right_product(fields, tables_ref[kind, 0], tables_ref[kind, 1], passes)
    return left_product(fields, tables_ref[other, 0], tables_ref[other, 1], passes)


def split_column(column, extent):
    return lax.shift_right_logical(column, extent.bit_length() - 1), column & (extent - 1)


def column_blocks(column, extent, columns):
    block, shift = split_column(column, extent)
    following = jnp.minimum(block + 1, columns // extent - 1)
    first = pl.multiple_of(block * extent, extent)
    return first, pl.multiple_of(following * extent, extent), shift


def kept_rows(shape, row, above):
    inside = lax.broadcasted_iota(jnp.int32, shape, 0) >= row
    return inside.astype(jnp.int32) == above


def exchange_kernel(
    sections,
    peers,
    offsets_hbm,
    layer_hbm,
    probe_hbm,
    intensity_hbm,
    tables_hbm,
    own_terms,
    near_terms,
    far_terms,
    near_places_hbm,
    far_places_hbm,
    own_places,
    near_places,
    far_places,
    layer,
    probe,
    intensity,
    intensity_out,
    intensity_in,
    tables,
    own_out,
    own_in,
    relay_out,
    relay_in,
    joined,
    rim_in,
    near_first,
    far_first,
    own_back,
    rim_back,
    waves_even,
    waves_odd,
    adjoint_even,
    adjoint_odd,
    load_sems,
    store_sems,
    place_send,
    place_recv,
    send_sems,
    intensity_recv,
    own_recv,
    relay_recv,
    rim_recv,
    near_recv,
    kept_sems,
    last_sems,
):
    waves, adjoint = ((waves_even, waves_odd), (adjoint_even, adjoint_odd))
    section = lax.axis_index("depth")
    scan = lax.axis_index("scan")
    even = jnp.where(lax.rem(scan, 2) == 0, 1, 0)
    odd = 1 - even
    partner = scan + even - odd
    far = scan - even + odd
    outward = scan - 2 * even + 2 * odd
    inward = scan + 2 * even - 2 * odd
    has_outward = (outward >= 0) & (outward < peers)
    has_inward = (inward >= 0) & (inward < peers)
    blocks, _, strip, extent = layer.shape
    owned = intensity.shape[0]
    last = owned - 1
    straight = max(0, owned - 2)

    loads = [
        pltpu.make_async_copy(source, target, load_sems.at[i])
        for i, (source, target) in enumerate(
            (
                (probe_hbm, probe),
                (intensity_hbm.at[pl.ds(section * owned, owned)], intensity),
                (tables_hbm, tables),
                (offsets_hbm, own_places),
            )
        )
    ]

    def layer_load(block):
        columns = pl.ds(pl.multiple_of(block * extent, extent), extent)
        return pltpu.make_async_copy(
            layer_hbm.at[:, :, columns], layer.at[block], load_sems.at[4]
        )

    def start_layer(block, carry):
        layer_load(block).start()
        return carry

    loads[3].start()
    lax.fori_loop(0, blocks, start_layer, 0)
    for load in loads[:3]:
        load.start()

    barrier = pltpu.get_barrier_semaphore()

    def greet(**device):
        pl.semaphore_signal(barrier, inc=1, device_id=device, device_id_type=MESH)

    def greet_section(step, carry):
        other = lax.rem(section + step, sections)
        greet(scan=partner, depth=other)

        @pl.when(step > 0)
        def _():
            greet(depth=other)

        @pl.when(has_outward)
        def _():
            greet(scan=outward, depth=other)

        @pl.when(has_inward)
        def _():
            greet(scan=inward, depth=other)

        return carry

    lax.fori_loop(0, sections, greet_section, 0)

    @pl.when(has_outward)
    def _():
        greet(scan=far)

    @pl.when(jnp.logical_not(has_inward))
    def _():
        relay_in[...] = jnp.zeros_like(relay_in)
        far_first[...] = jnp.zeros_like(far_first)

    greeted = (
        2 * sections
        - 1
        + jnp.where(has_outward, sections + 1, 0)
        + jnp.where(has_inward, sections, 0)
    )
    loads[3].wait()
    pl.semaphore_wait(barrier, greeted)

    def remote(source, target, send, recv, device):
        return pltpu.make_async_remote_copy(
            src_ref=source,
            dst_ref=target,
            send_sem=send,
            recv_sem=recv,
            device_id=device,
            device_id_type=MESH,
        )

    near_place_copy = remote(
        own_places, near_places, place_send.at[0], place_recv.at[0], {"scan": partner}
    )
    far_place_copy = remote(
        own_places, far_places, place_send.at[1], place_recv.at[1], {"scan": far}
    )
    near_place_copy.start()

    @pl.when(has_outward)
    def _():
        far_place_copy.start()

    @pl.when(jnp.logical_not(has_outward))
    def _():
        def clear(index, carry):
            far_places[0, index] = 0
            far_places[1, index] = 0
            return carry

        lax.fori_loop(0, far_places.shape[1], clear, 0)

    def own_copy(owner, sender, first, count):
        return remote(
            own_out.at[owner, pl.ds(first, count)],
            own_in.at[sender, pl.ds(first, count)],
            send_sems.at[0],
            own_recv.at[first],
            {"scan": partner, "depth": owner},
        )

    def intensity_copy(first, count):
        return remote(
            intensity_out.at[pl.ds(first, count)],
            intensity_in.at[pl.ds(first, count)],
            send_sems.at[1],
            intensity_recv.at[first],
            {"scan": partner},
        )

    def relay_copy(place):
        return remote(
            relay_out.at[place],
            relay_in.at[place],
            send_sems.at[2],
            relay_recv.at[place],
            {"scan": outward},
        )

    def far_first_copy(owner):
        return remote(
            relay_out.at[0, owner],
            far_first.at[section],
            send_sems.at[2],
            relay_recv.at[0],
            {"scan": outward, "depth": owner},
        )

    def near_first_copy(owner):
        return remote(
            joined.at[0, owner],
            near_first.at[section],
            send_sems.at[3],
            rim_recv.at[0],
            {"depth": owner},
        )

    def rim_copy(owner, place):
        return remote(
            joined.at[place, owner],
            rim_in.at[place, section],
            send_sems.at[3],
            rim_recv.at[place],
            {"depth": owner},
        )

    def own_back_copy(target, place):
        return remote(
            own_back.at[place, target],
            own_terms.at[place, section],
            send_sems.at[4],
            last_sems.at[0],
            {"scan": partner, "depth": target},
        )

    def rim_back_copy(target, place):
        return remote(
            rim_back.at[place, target],
            near_terms.at[place, section],
            send_sems.at[5],
            near_recv.at[place],
            {"depth": target},
        )

    def keep_near(place):
        return pltpu.make_async_copy(
            rim_back.at[place, section], near_terms.at[place, section], kept_sems.at[place]
        )

    def onward_copy(place):
        return remote(
            near_terms.at[place],
            far_terms.at[place],
            send_sems.at[6],
            last_sems.at[1],
            {"scan": inward},
        )

    def far_last_copy(target, place):
        return remote(
            rim_back.at[place, target],
            far_terms.at[place, section],
            send_sems.at[6],
            last_sems.at[1],
            {"scan": inward, "depth": target},
        )

    def sent(index, ref):
        remote(ref, ref, send_sems.at[index], last_sems.at[0], {"scan": partner}).wait_send()

    def arrived(ref, sem):
        remote(ref, ref, send_sems.at[0], sem, {"scan": partner}).wait_recv()

    others = pl.ds(0, sections - 1)

    lanes = lax.broadcasted_iota(jnp.int32, (strip, extent), 1)

    def cut(column):
        first, shift = split_column(column, extent)
        second = jnp.minimum(first + 1, blocks - 1)
        ahead = lanes >= shift
        return [jnp.where(ahead, layer[first, part], layer[second, part]) for part in range(2)]

    order = [lax.rem(section + 1 + step, sections) for step in range(sections)]

    loads[1].wait()

    pltpu.make_async_copy(layer, layer, load_sems.at[4]).wait()

    def cut_own(place):
        for owner in order:
            for part, half in enumerate(cut(own_places[1, owner * owned + place])):
                own_out[owner, place, part] = half.astype(jnp.bfloat16)

    def send_own(first, count):
        lax.fori_loop(first, first + count, lambda place, carry: (cut_own(place), carry)[1], 0)
        for owner in order:
            own_copy(owner, section, first, count).start()

    def send_intensity(first, count):
        picked = pl.ds(first, count)
        intensity_out[picked] = intensity[picked].astype(jnp.bfloat16)
        intensity_copy(first, count).start()

    def cut_far(place):
        for owner in order:
            index = owner * owned + place
            keep = kept_rows((strip, extent), far_places[0, index] - (far - 1) * strip, odd)
            for part, half in enumerate(cut(far_places[1, index])):
                relay_out[place, owner, part] = jnp.where(keep, half, 0.0).astype(jnp.bfloat16)

    def send_relay(place, carry):
        cut_far(place)
        relay_copy(place).start()
        return carry

    def near_kept(index):
        row = near_places[0, index] - (partner - 1) * strip
        return kept_rows((strip, extent), row, even)

    def send_near_first():
        for owner in order:
            for part, half in enumerate(cut(near_places[1, owner * owned])):
                joined[0, owner, part] = half.astype(jnp.bfloat16)
        near_first[section] = joined[0, section]
        for owner in order[:-1]:
            near_first_copy(owner).start()

    def await_relay(place):
        @pl.when(has_inward)
        def _():
            arrived(relay_in.at[place], relay_recv.at[place])

    def send_rim(owner, place):
        index = owner * owned + place
        keep = near_kept(index)
        for part, half in enumerate(cut(near_places[1, index])):
            passed = relay_in[place, owner, part].astype(jnp.float32)
            joined[place, owner, part] = jnp.where(keep, half, passed).astype(jnp.bfloat16)

        @pl.when(owner != section)
        def _():
            rim_copy(owner, place).start()

        @pl.when(owner == section)
        def _():
            rim_in[place, section] = joined[place, section]

    chunks = [(first, 1) for first in range(min(owned, 2))]
    if owned > 2:
        chunks.append((2, owned - 2))
    for first, count in chunks:
        send_own(first, count)
        send_intensity(first, count)

    @pl.when(has_outward)
    def _():
        far_place_copy.wait()
        cut_far(0)
        for owner in order:
            far_first_copy(owner).start()

    near_place_copy.wait()
    place_stores = [
        pltpu.make_async_copy(source, target, store_sems.at[i])
        for i, (source, target) in enumerate(
            ((near_places, near_places_hbm), (far_places, far_places_hbm))
        )
    ]
    for place_store in place_stores:
        place_store.start()
    send_near_first()

    @pl.when(has_outward)
    def _():
        lax.fori_loop(1, owned, send_relay, 0)

    loads[0].wait()
    loads[2].wait()

    def join_first():
        arrived(near_first.at[others], rim_recv.at[0])

        @pl.when(has_inward)
        def _():
            arrived(far_first, relay_recv.at[0])

        keep = near_kept(section * owned)

        def join_slice(slice_index, carry):
            for part in range(2):
                here = near_first[slice_index, part].astype(jnp.float32)
                passed = far_first[slice_index, part].astype(jnp.float32)
                rim_in[0, slice_index, part] = jnp.where(keep, here, passed).astype(jnp.bfloat16)
            return carry

        lax.fori_loop(0, sections, join_slice, 0)

    def patch(slice_index, place):
        return tuple(
            jnp.concatenate(
                [own_in[slice_index, place, part], rim_in[place, slice_index, part]], axis=0
            ).astype(jnp.float32)
            for part in range(2)
        )

    def stored(ref, *place):
        return (ref[(*place, 0)], ref[(*place, 1)])

    def store(ref, place, field):
        for part in range(2):
            ref[(*place, part)] = field[part]

    final = sections - 1

    def await_near(place):
        arrived(near_terms.at[place, others], near_recv.at[place])
        keep_near(place).wait()

    def prepare(step, place):
        if place is not None:
            if isinstance(step, int):
                if step == 0:
                    await_relay(place)
            else:
                pl.when(step == 0)(lambda: await_relay(place))

            send_rim(lax.rem(section + 1 + step, sections), place)

    def begin(place):
        if place == 0:
            join_first()
        else:
            arrived(rim_in.at[place, others], rim_recv.at[place])
        index = section * owned + place
        down = near_places[0, index] - (partner - 2) * strip
        right = lax.rem(near_places[1, index], extent)
        rolled = [pltpu.roll(probe[part], lax.rem(down, extent), 0) for part in range(2)]
        store(waves[place % 2], (0,), [pltpu.roll(value, right, 1) for value in rolled])
        for first, count in chunks:
            if first == place:
                arrived(own_in.at[:, pl.ds(first, count)], own_recv.at[first])

    def excite(place, slice_index):
        return times(patch(slice_index, place), stored(waves[place % 2], slice_index))

    def forward(place, slice_index):
        return transform([excite(place, slice_index)], tables, HOP)[0]

    def turn(place):
        (real, imag), = transform([excite(place, final)], tables, FOURIER)
        for first, count in chunks:
            if first == place:
                intensity_copy(first, count).wait_recv()
        misfit = real * real + imag * imag - intensity_in[place].astype(jnp.float32)
        driven = (misfit * real, misfit * imag)
        store(adjoint[place % 2], (), transform([driven], tables, FOURIER_CONJ)[0])

    def form(place, slice_index):
        term = conj_times(stored(waves[place % 2], slice_index), stored(adjoint[place % 2]))
        for part in range(2):
            value = term[part].astype(jnp.bfloat16)
            own_back[place, slice_index, part] = value[:strip]
            rim_back[place, slice_index, part] = value[strip:]

    def give(place, slice_index):
        if place >= straight:

            @pl.when(has_inward)
            def _():
                far_last_copy(slice_index, place).start()

        @pl.when(slice_index != section)
        def _():
            rim_back_copy(slice_index, place).start()

        @pl.when(slice_index == section)
        def _():
            keep_near(place).start()

        own_back_copy(slice_index, place).start()

    def backward(place, slice_index):
        masked = conj_times(patch(slice_index, place), stored(adjoint[place % 2]))
        return transform([masked], tables, HOP_CONJ, passes=1)[0]

    def run_position(place, early, late):
        begin(place)

        def forward_step(index, carry):
            store(waves[place % 2], (index + 1,), forward(place, index))
            return carry

        lax.fori_loop(0, final, forward_step, 0, unroll=True)
        for index in range(sections):
            prepare(index, early)
        turn(place)

        def backward_step(index, carry):
            form(place, final - index)
            behind = backward(place, final - index)
            give(place, final - index)
            store(adjoint[place % 2], (), behind)
            prepare(index, late)
            return carry

        lax.fori_loop(0, final, backward_step, 0)
        form(place, 0)
        give(place, 0)
        if 0 < place <= straight:
            await_near(place - 1)

            @pl.when(has_inward)
            def _():
                onward_copy(place - 1).start()

        prepare(final, late)

    joins = [*range(1, owned), *[None] * (owned + 1)]
    for place in range(owned):
        run_position(place, *joins[2 * place : 2 * place + 2])

    for place in range(straight, owned):
        await_near(place)

    for place_store in place_stores:
        place_store.wait()

    for index, ref in (
        (0, own_out),
        (1, intensity_out),
        (3, joined.at[:, others]),
        (4, own_back),
        (5, rim_back.at[:, others]),
    ):
        sent(index, ref)

    arrived(own_terms, last_sems.at[0])

    @pl.when(has_outward)
    def _():
        sent(2, relay_out)
        arrived(far_terms, last_sems.at[1])

    @pl.when(has_inward)
    def _():
        sent(6, far_terms)


def exchange(sections, peers, offsets, layer, probe, intensity):
    positions, extent = (intensity.shape[0], intensity.shape[-1])
    strip, columns = layer.shape[1:]
    blocks = columns // extent
    owned = positions // sections
    hbm = pl.BlockSpec(memory_space=pltpu.HBM)
    tables = jnp.asarray(block_tables(extent))
    by_place = (owned, sections, 2, strip, extent)
    by_owner = (sections, owned, 2, strip, extent)
    first = (sections, 2, strip, extent)
    buffers = (by_owner, by_owner, by_place, by_place, by_place, by_place, first, first)
    buffers += (by_place, by_place)
    per_place = pltpu.SemaphoreType.DMA((owned,))
    out = pl.pallas_call(
        functools.partial(exchange_kernel, sections, peers),
        out_shape=[jax.ShapeDtypeStruct(by_place, jnp.bfloat16)] * 3
        + [jax.ShapeDtypeStruct((2, positions), jnp.int32)] * 2,
        in_specs=[hbm] * 5,
        out_specs=[hbm] * 5,
        scratch_shapes=[
            *[pltpu.SMEM((2, positions), jnp.int32)] * 3,
            pltpu.VMEM((blocks, 2, strip, extent), jnp.float32),
            pltpu.VMEM(probe.shape, jnp.float32),
            pltpu.VMEM((owned, extent, extent), jnp.float32),
            pltpu.VMEM((owned, extent, extent), jnp.bfloat16),
            pltpu.VMEM((owned, extent, extent), jnp.bfloat16),
            pltpu.VMEM(tables.shape, jnp.bfloat16),
            *[pltpu.VMEM(shape, jnp.bfloat16) for shape in buffers],
            *[pltpu.VMEM((sections, 2, extent, extent), jnp.float32)] * 2,
            *[pltpu.VMEM((2, extent, extent), jnp.float32)] * 2,
            pltpu.SemaphoreType.DMA((5,)),
            pltpu.SemaphoreType.DMA((2,)),
            pltpu.SemaphoreType.DMA((2,)),
            pltpu.SemaphoreType.DMA((2,)),
            pltpu.SemaphoreType.DMA((7,)),
            *[per_place] * 6,
            pltpu.SemaphoreType.DMA((2,)),
        ],
        compiler_params=pltpu.CompilerParams(
            collective_id=0, has_side_effects=True, vmem_limit_bytes=56 * 1024 * 1024
        ),
        name="exchange",
    )(offsets, layer, probe, intensity, tables)
    return out[:3], [offsets, *out[3:]]


def scatter_kernel(
    peers,
    sections,
    own_places_hbm,
    near_places_hbm,
    far_places_hbm,
    own_hbm,
    near_hbm,
    far_hbm,
    out_hbm,
    own_places,
    near_places,
    far_places,
    own_ref,
    near_ref,
    far_ref,
    total_real,
    total_imag,
    load_sems,
    store_sems,
):
    scan = lax.axis_index("scan")
    positions = own_ref.shape[0]
    strip, extent = own_ref.shape[2:]
    totals = (total_real, total_imag)
    columns = total_real.shape[1]
    even = jnp.where(lax.rem(scan, 2) == 0, 1, 0)
    odd = 1 - even
    partner = scan + even - odd
    far = scan - even + odd
    has_far = (far >= 0) & (far < peers)

    loads = [
        pltpu.make_async_copy(source, target, load_sems.at[i])
        for i, (source, target) in enumerate(
            (
                (own_places_hbm, own_places),
                (near_places_hbm, near_places),
                (far_places_hbm, far_places),
                (own_hbm, own_ref),
                (near_hbm, near_ref),
                (far_hbm, far_ref),
            )
        )
    ]
    for load in loads:
        load.start()
    for total in totals:
        total[...] = jnp.zeros_like(total)
    lanes = lax.broadcasted_iota(jnp.int32, (strip, extent), 1)

    def add(source, index, column, keep):
        first, second, shift = column_blocks(column, extent, columns)
        ahead = lanes >= shift
        terms = [source[index, part].astype(jnp.float32) for part in range(2)]
        if keep is not None:
            terms = [jnp.where(keep, term, 0.0) for term in terms]
        for start, chosen in ((first, ahead), (second, jnp.logical_not(ahead))):
            place = (slice(None), pl.ds(start, extent))
            sums = [
                total[place] + jnp.where(chosen, term, 0.0) for total, term in zip(totals, terms)
            ]
            for total, value in zip(totals, sums):
                total[place] = value

    def add_all(source, places, neighbour, above):
        def step(index, carry):
            owner, place = (lax.rem(index, sections), lax.div(index, sections))
            position = owner * (positions // sections) + place
            row = places[0, position] - (neighbour - 1) * strip
            keep = None if above is None else kept_rows((strip, extent), row, above)
            add(source, index, places[1, position], keep)
            return carry

        lax.fori_loop(0, positions, step, 0, unroll=8)

    loads[0].wait()
    loads[3].wait()
    add_all(own_ref, own_places, scan, None)
    loads[1].wait()
    loads[4].wait()
    add_all(near_ref, near_places, partner, even)
    loads[2].wait()
    loads[5].wait()

    @pl.when(has_far)
    def _():
        add_all(far_ref, far_places, far, odd)

    stores = [
        pltpu.make_async_copy(total, out_hbm.at[part], store_sems.at[part])
        for part, total in enumerate(totals)
    ]
    for store in stores:
        store.start()
    for store in stores:
        store.wait()


def scatter(peers, sections, places, terms, strip, columns):
    hbm = pl.BlockSpec(memory_space=pltpu.HBM)
    terms = [term.reshape(-1, *term.shape[-3:]) for term in terms]
    return pl.pallas_call(
        functools.partial(scatter_kernel, peers, sections),
        out_shape=jax.ShapeDtypeStruct((2, strip, columns), jnp.float32),
        in_specs=[hbm] * 6,
        out_specs=hbm,
        scratch_shapes=[pltpu.SMEM(place.shape, place.dtype) for place in places]
        + [pltpu.VMEM(term.shape, term.dtype) for term in terms]
        + [
            pltpu.VMEM((strip, columns), jnp.float32),
            pltpu.VMEM((strip, columns), jnp.float32),
            pltpu.SemaphoreType.DMA((6,)),
            pltpu.SemaphoreType.DMA((2,)),
        ],
        compiler_params=pltpu.CompilerParams(vmem_limit_bytes=56 * 1024 * 1024),
        name="scatter",
    )(*places, *terms)


def shards(peers, sections, object_slices, probe_wave, offsets, intensity):
    layer = object_slices[0]
    strip, columns = layer.shape[1:]
    places = offsets.T
    terms, taken = exchange(sections, peers, places, layer, probe_wave, intensity)
    return scatter(peers, sections, taken, terms, strip, columns)[None]


def solution(mesh):
    in_specs = (P("depth", None, "scan", None), P(), P("scan", None), P("scan", None, None))
    out_specs = P("depth", None, "scan", None)
    body = functools.partial(shards, mesh.shape["scan"], mesh.shape["depth"])
    return jax.shard_map(body, mesh=mesh, in_specs=in_specs, out_specs=out_specs, check_vma=False)
```
